512 devices in a mesh: section: 16 (over y, z_hi), tok: 32 (over x, z_lo, core).
Axes of the slice: x: 4, y: 8, z: 8 (z_hi: 2, z_lo: 4; z = z_hi * 4 + z_lo), core: 2. Of those that a mesh axis runs over, the one named last changes fastest.
Arguments:
- stream_one: float32 [16, 2048, 1024], P('section', 'tok'), may hold values from -6 to 6
- stream_two: float32 [16, 2048, 1024], P('section', 'tok'), may hold values from -6 to 6
- grad_one: bfloat16 [16, 2048, 1024], P('section', 'tok'), may hold values from -6 to 6
- grad_two: bfloat16 [16, 2048, 1024], P('section', 'tok'), may hold values from -6 to 6
- sensor_ids: int32 [16, 128], P('section'), may hold values from 0 to 7
- block_order: int32 [16, 128], P('section'), may hold values from 0 to 127, each once within a row
- qkv_weight: bfloat16 [16, 1024, 3072], P('section', 'tok'), may hold values from -0.1875 to 0.1875
- out_weight: bfloat16 [16, 1024, 1024], P('section', 'tok'), may hold values from -0.1875 to 0.1875
- attn_gain: float32 [16, 1024], P('section'), may hold values from 0.5 to 1.5
- adapt_gain: float32 [16, 1024], P('section'), may hold values from 0.5 to 1.5
- logit_scale: float32 [16, 8], P('section'), may hold values from 2 to 12
- distance_slope: float32 [16, 8], P('section'), may hold values from 0.02 to 0.6
- adapt_down: bfloat16 [16, 1024, 128], P('section'), may hold values from -0.1875 to 0.1875
- adapt_up: bfloat16 [16, 128, 1024], P('section'), may hold values from -1.5 to 1.5
Outputs:
- inverse_one: float32 [16, 2048, 1024], P('section', 'tok')
- inverse_two: float32 [16, 2048, 1024], P('section', 'tok')
- cot_one: bfloat16 [16, 2048, 1024], P('section', 'tok')
- cot_two: bfloat16 [16, 2048, 1024], P('section', 'tok')
- down_grad: bfloat16 [16, 1024, 128], P('section')
- up_grad: bfloat16 [16, 128, 1024], P('section')
The draws below stay inside these ranges and needn't reach their ends.
Inputs may be any that keep to these rules, and one draw needn't show every extreme that they name: `block_order`: each row names every block place once.
All inputs are finite; a program needn't handle non-finite values.
Results may differ from the reference program's by a relative error of at most 0.02.
Values may be sent and summed in bfloat16 or wider, within the bound.
A program may use at most 64 MiB of HBM per device.

```python
import math
import jax
import jax.numpy as jnp
from jax import lax

D = 1024
HEADS = 8
HS = 128
SENSORS = 8
RANK = 16
BLOCK = 16
TOK_DEV = 64
WIN = 32
TOKENS = 2048
NBLK = 128
SR = 128
SECTIONS = 16
N_TOK = 32


def place_ends(values, own_key, least, top_value):
    index_at = [jax.random.randint(jax.random.fold_in(own_key, axis), (), 0, length) for axis, length in enumerate(values.shape)]
    widest = values.shape.index(max(values.shape))
    neighbour = index_at[:widest] + [(index_at[widest] + 1) % values.shape[widest]] + index_at[widest + 1:]
    return values.at[tuple(index_at)].set(least).at[tuple(neighbour)].set(top_value)


def block_scale(own_key, dims, shards, smallest, top_value):
    level, own = 1.0, jax.random.fold_in(own_key, 6)
    for dim, shards_of in shards:
        draws = jnp.exp(jax.random.uniform(jax.random.fold_in(own, dim), (shards_of,), jnp.float32, smallest / len(shards), top_value / len(shards)))
        level = level * jnp.repeat(draws, dims[dim] // shards_of).reshape([-1 if axis == dim else 1 for axis in range(len(dims))])
    return level


def gaussian(own_key, extent, scale, limit, cuts=(), held_as=jnp.bfloat16):
    array = jax.random.normal(own_key, extent, jnp.float32) * scale
    if len(cuts) > 0:
        array = block_scale(own_key, extent, cuts, -0.22, 0.18) * array
    return jnp.clip(array, min=-limit, max=limit).astype(held_as)


def setup_inputs(seed: int = 0) -> dict:
    seeds = jax.random.split(jax.random.key(seed), 15)
    stream_one = gaussian(seeds[0], (SECTIONS, TOKENS, D), 1.0, 6.0, ((0, 16), (1, 32)), jnp.float32)
    stream_two = gaussian(seeds[1], (SECTIONS, TOKENS, D), 1.0, 6.0, ((0, 16), (1, 32)), jnp.float32)
    grad_one = gaussian(seeds[2], (SECTIONS, TOKENS, D), 1.0, 6.0, ((0, 16), (1, 32)))
    grad_two = gaussian(seeds[3], (SECTIONS, TOKENS, D), 1.0, 6.0, ((0, 16), (1, 32)))
    sensor_ids = place_ends(jax.random.randint(seeds[4], (SECTIONS, NBLK), 0, SENSORS), jax.random.fold_in(seeds[4], 1), 0, SENSORS - 1).astype(jnp.int32)
    block_order = jax.vmap(lambda own: jax.random.permutation(own, NBLK))(jax.random.split(seeds[5], SECTIONS)).reshape((SECTIONS, NBLK)).astype(jnp.int32)
    qkv_weight = gaussian(seeds[6], (SECTIONS, D, 3 * D), D ** -0.5, 0.1875, ((0, 16), (1, 32)))
    out_weight = gaussian(seeds[7], (SECTIONS, D, D), D ** -0.5, 0.1875, ((0, 16), (1, 32)))
    attn_gain = jnp.clip(1.0 + 0.1 * jax.random.normal(seeds[8], (SECTIONS, D), jnp.float32), 0.5, 1.5)
    adapt_gain = jnp.clip(1.0 + 0.1 * jax.random.normal(seeds[9], (SECTIONS, D), jnp.float32), 0.5, 1.5)
    logit_scale = jnp.clip(jnp.exp(math.log(12.0) - 1.7917595 * jax.random.uniform(seeds[10], (SECTIONS, HEADS), jnp.float32) ** block_scale(seeds[10], (SECTIONS, HEADS), ((0, 16),), -0.2, 0.2)), 2.0, 12.0)
    distance_slope = jnp.clip(jnp.exp(math.log(0.6) - 3.4011974 * jax.random.uniform(seeds[11], (SECTIONS, HEADS), jnp.float32) ** block_scale(seeds[11], (SECTIONS, HEADS), ((0, 16),), -0.2, 0.2)), 0.02, 0.6)
    adapt_down = gaussian(seeds[12], (SECTIONS, D, SR), D ** -0.5, 0.1875, ((0, 16),))
    adapt_up = gaussian(seeds[13], (SECTIONS, SR, D), RANK ** -0.5, 1.5, ((0, 16),))
    return {"stream_one": stream_one, "stream_two": stream_two, "grad_one": grad_one, "grad_two": grad_two, "sensor_ids": sensor_ids, "block_order": block_order, "qkv_weight": qkv_weight, "out_weight": out_weight, "attn_gain": attn_gain, "adapt_gain": adapt_gain, "logit_scale": logit_scale, "distance_slope": distance_slope, "adapt_down": adapt_down, "adapt_up": adapt_up}


def layer_norm(values, gain):
    centre = lax.optimization_barrier(jnp.mean(values, axis=-1, keepdims=True))
    centred = values - centre
    inverse = lax.rsqrt(lax.optimization_barrier(jnp.mean(centred * centred, axis=-1, keepdims=True)) + 1e-05)
    scaled = centred * inverse
    return (scaled * gain, scaled, inverse)

def norm_back(upstream, gain, scaled, inverse):
    inner = upstream * gain
    return inverse * (inner - lax.optimization_barrier(jnp.mean(inner, axis=-1, keepdims=True)) - scaled * lax.optimization_barrier(jnp.mean(inner * scaled, axis=-1, keepdims=True)))

def gelu_exact(values):
    return values * 0.5 * (1.0 + jax.scipy.special.erf(values * 0.7071067811865476))

def gelu_slope(values):
    return 0.5 * (1.0 + jax.scipy.special.erf(values * 0.7071067811865476)) + values * jnp.exp(-0.5 * values * values) * 0.3989422804014327

def sensor_columns(tok_sensor, columns):
    column_owner = jnp.arange(columns, dtype=jnp.int32) // RANK
    return (column_owner[None, :] == tok_sensor[:, None]).astype(jnp.float32)

def adapter_pass(top_in, bottom_in, top_cot, bottom_cot, sensor_mask, gain, down, upper):
    normed, scaled, inverse = layer_norm(top_in, gain)
    adapt_in = normed.astype(jnp.bfloat16)
    hidden_pre = jnp.dot(adapt_in, down, preferred_element_type=jnp.float32) * sensor_mask
    hidden = gelu_exact(hidden_pre).astype(jnp.bfloat16)
    bottom_out = bottom_in - jnp.dot(hidden, upper, preferred_element_type=jnp.float32)
    hidden_cot = jnp.dot(bottom_cot, upper.T, preferred_element_type=jnp.float32)
    hidden_grad = (sensor_mask * gelu_slope(hidden_pre) * hidden_cot).astype(jnp.bfloat16)
    grad_down = jnp.dot(adapt_in.T, hidden_grad, preferred_element_type=jnp.float32)
    grad_up = jnp.dot(hidden.T, bottom_cot, preferred_element_type=jnp.float32)
    normed_grad = jnp.dot(hidden_grad, down.T, preferred_element_type=jnp.float32)
    top_grad = top_cot.astype(jnp.float32) + norm_back(normed_grad, gain, scaled, inverse)
    return (bottom_out, top_grad, grad_down, grad_up)

def window_mask(begin, total):
    query_idx = jnp.arange(TOK_DEV, dtype=jnp.int32)[:, None]
    key_idx = jnp.arange(TOK_DEV + 2 * WIN, dtype=jnp.int32)[None, :]
    global_key = begin - WIN + key_idx
    allowed = (key_idx >= query_idx) & (key_idx <= query_idx + 2 * WIN) & (global_key >= 0) & (global_key < total)
    return allowed.astype(jnp.float32)

def attend(query_bf, key_window, query_pos, key_pos, allowed, scale, slope):
    products = jnp.einsum('thd,shd->hts', query_bf.astype(jnp.float32), key_window.astype(jnp.float32))
    distance = jnp.log1p(jnp.abs(query_pos[:, None] - key_pos[None, :]))
    score = products * (scale / HS)[:, None, None] - slope[:, None, None] * distance[None]
    weights = jnp.exp(score) * allowed[None]
    return weights / lax.optimization_barrier(jnp.sum(weights, axis=-1, keepdims=True))

def attend_back(attention, query_bf, key_window, value_window, mixed_grad, scale):
    attention_bf = attention.astype(jnp.bfloat16).astype(jnp.float32)
    value_cot = jnp.einsum('thd,shd->hts', mixed_grad.astype(jnp.float32), value_window.astype(jnp.float32))
    centre = lax.optimization_barrier(jnp.sum(attention * value_cot, axis=-1, keepdims=True))
    score_grad = (attention * (value_cot - centre) * (scale / HS)[:, None, None]).astype(jnp.bfloat16).astype(jnp.float32)
    value_grad = jnp.einsum('hts,thd->shd', attention_bf, mixed_grad.astype(jnp.float32))
    query_grad = jnp.einsum('hts,shd->thd', score_grad, key_window.astype(jnp.float32))
    key_grad = jnp.einsum('hts,thd->shd', score_grad, query_bf.astype(jnp.float32))
    return (query_grad, key_grad, value_grad)

def unit_back(unit_grad, unit, scale_row):
    return scale_row * (unit_grad - unit * lax.optimization_barrier(jnp.mean(unit_grad * unit, axis=-1, keepdims=True)))

def tick(top_in, bottom_in, top_cot, bottom_cot, sensor, order, w_qkv, w_out, gain_f, gain_g, scale, slope, down, upper):
    total = top_in.shape[0]
    span = TOK_DEV + 2 * WIN
    tok_sensor = jnp.repeat(sensor, BLOCK, total_repeat_length=total)
    sensor_mask = sensor_columns(tok_sensor, down.shape[1])
    bottom_out, top_grad, grad_down, grad_up = adapter_pass(top_in, bottom_in, top_cot, bottom_cot, sensor_mask, gain_g, down, upper)
    normed, scaled, inverse = layer_norm(bottom_out, gain_f)
    projected = jnp.dot(normed.astype(jnp.bfloat16), w_qkv, preferred_element_type=jnp.float32)
    queries = projected[:, :D].reshape(total, HEADS, HS)
    keys_all = projected[:, D:2 * D].reshape(total, HEADS, HS)
    values = projected[:, 2 * D:].reshape(total, HEADS, HS)
    query_scale = lax.rsqrt(lax.optimization_barrier(jnp.mean(queries * queries, axis=-1, keepdims=True)) + 1e-06)
    key_scale = lax.rsqrt(lax.optimization_barrier(jnp.mean(keys_all * keys_all, axis=-1, keepdims=True)) + 1e-06)
    query_unit = queries * query_scale
    key_unit = keys_all * key_scale
    query_bf = query_unit.astype(jnp.bfloat16)
    key_bf = key_unit.astype(jnp.bfloat16)
    value_bf = values.astype(jnp.bfloat16)
    positions = jnp.repeat(order, BLOCK, total_repeat_length=total).astype(jnp.float32)
    key_pad = jnp.pad(key_bf, ((WIN, WIN), (0, 0), (0, 0)))
    value_pad = jnp.pad(value_bf, ((WIN, WIN), (0, 0), (0, 0)))
    pos_pad = jnp.pad(positions, (WIN, WIN))
    block_ids = jnp.arange(N_TOK, dtype=jnp.int32)

    def pieces(block_idx):
        begin = (block_idx * TOK_DEV).astype(jnp.int32)
        query_blk = lax.dynamic_slice_in_dim(query_bf, begin, TOK_DEV, 0)
        key_blk = lax.dynamic_slice_in_dim(key_pad, begin, span, 0)
        value_blk = lax.dynamic_slice_in_dim(value_pad, begin, span, 0)
        query_pos = lax.dynamic_slice_in_dim(positions, begin, TOK_DEV, 0)
        key_pos = lax.dynamic_slice_in_dim(pos_pad, begin, span, 0)
        attention = attend(query_blk, key_blk, query_pos, key_pos, window_mask(begin, total), scale, slope)
        return (begin, query_blk, key_blk, value_blk, attention)

    def forward_block(block_idx):
        begin, query_blk, key_blk, value_blk, attention = pieces(block_idx)
        mixed = jnp.einsum('hts,shd->thd', attention.astype(jnp.bfloat16).astype(jnp.float32), value_blk.astype(jnp.float32))
        return mixed.astype(jnp.bfloat16)
    mixed_all = lax.map(forward_block, block_ids).reshape(total, D)
    top_out = top_in - jnp.dot(mixed_all, w_out, preferred_element_type=jnp.float32)
    mixed_grad = jnp.dot(top_grad.astype(jnp.bfloat16), w_out.T, preferred_element_type=jnp.float32).astype(jnp.bfloat16).reshape(total, HEADS, HS)

    def backward_block(block_idx):
        begin, query_blk, key_blk, value_blk, attention = pieces(block_idx)
        grad_blk = lax.dynamic_slice_in_dim(mixed_grad, begin, TOK_DEV, 0)
        query_grad, key_grad, value_grad = attend_back(attention, query_blk, key_blk, value_blk, grad_blk, scale)
        stacked = jnp.concatenate([key_grad.reshape(span, D), value_grad.reshape(span, D)], axis=1)
        return (query_grad, stacked)
    query_grads, contrib = lax.map(backward_block, block_ids)
    own = contrib[:, WIN:WIN + TOK_DEV]
    empty = jnp.zeros((1, WIN, 2 * D), jnp.float32)
    from_left = jnp.concatenate([empty, contrib[:-1, WIN + TOK_DEV:]], axis=0)
    from_right = jnp.concatenate([contrib[1:, :WIN], empty], axis=0)
    own = own.at[:, :WIN].add(from_left)
    own = own.at[:, TOK_DEV - WIN:].add(from_right)
    own = own.reshape(total, 2 * D)
    key_unit_grad = own[:, :D].reshape(total, HEADS, HS)
    value_grad_all = own[:, D:]
    query_unit_grad = query_grads.reshape(total, HEADS, HS)
    query_full = unit_back(query_unit_grad, query_unit, query_scale).reshape(total, D)
    key_full = unit_back(key_unit_grad, key_unit, key_scale).reshape(total, D)
    joined = jnp.concatenate([query_full, key_full, value_grad_all], axis=1).astype(jnp.bfloat16)
    normed_grad = jnp.dot(joined, w_qkv.T, preferred_element_type=jnp.float32)
    bottom_grad = bottom_cot.astype(jnp.float32) + norm_back(normed_grad, gain_f, scaled, inverse)
    return (top_out, bottom_out, top_grad.astype(jnp.bfloat16), bottom_grad.astype(jnp.bfloat16), grad_down, grad_up)

def shifted(values):
    return jnp.concatenate([values[1:], jnp.zeros_like(values[:1])], axis=0)

def reference(stream_one, stream_two, grad_one, grad_two, sensor_ids, block_order, qkv_weight, out_weight, attn_gain, adapt_gain, logit_scale, distance_slope, adapt_down, adapt_up):
    section_ids = jnp.arange(SECTIONS, dtype=jnp.int32)

    def first_tick(index):
        return tick(stream_one[index], stream_two[index], grad_one[index], grad_two[index], sensor_ids[index], block_order[index], qkv_weight[index], out_weight[index], attn_gain[index], adapt_gain[index], logit_scale[index], distance_slope[index], adapt_down[index], adapt_up[index])
    first = lax.map(first_tick, section_ids)
    next_top = shifted(first[0])
    next_bottom = shifted(first[1])
    next_top_cot = shifted(first[2])
    next_bottom_cot = shifted(first[3])
    next_sensor = shifted(sensor_ids)
    next_order = shifted(block_order)

    def second_tick(index):
        return tick(next_top[index], next_bottom[index], next_top_cot[index], next_bottom_cot[index], next_sensor[index], next_order[index], qkv_weight[index], out_weight[index], attn_gain[index], adapt_gain[index], logit_scale[index], distance_slope[index], adapt_down[index], adapt_up[index])
    second = lax.map(second_tick, section_ids)
    down_grad = (first[4] + second[4]).astype(jnp.bfloat16)
    up_grad = (first[5] + second[5]).astype(jnp.bfloat16)
    return (second[0], second[1], second[2], second[3], down_grad, up_grad)
```

```python
import functools

import jax
import jax.numpy as jnp
from jax import lax
from jax.experimental import pallas as pl
from jax.experimental.pallas import tpu as pltpu
from jax.sharding import PartitionSpec as P

RANK = 16
BLOCK = 16
WIN = 32
HS = 128
NX = 4
MESH = pl.DeviceIdType.MESH
F32 = jnp.float32
BF16 = jnp.bfloat16


def dot(left, right):
    return jnp.dot(left, right, preferred_element_type=F32)


def dot_last(left, right):
    return lax.dot_general(left, right, (((1,), (1,)), ((), ())), preferred_element_type=F32)


def dot_first(left, right):
    return lax.dot_general(left, right, (((0,), (0,)), ((), ())), preferred_element_type=F32)


def layer_norm(values):
    centred = values - jnp.mean(values, axis=-1, keepdims=True)
    inverse = lax.rsqrt(jnp.mean(centred * centred, axis=-1, keepdims=True) + 1e-05)
    return centred * inverse, inverse


def norm_back(upstream, gain, scaled, inverse):
    inner = upstream * gain
    mean_one = jnp.mean(inner, axis=-1, keepdims=True)
    mean_two = jnp.mean(inner * scaled, axis=-1, keepdims=True)
    return inverse * (inner - mean_one - scaled * mean_two)


def phi(values):
    return 0.5 * (1.0 + lax.erf(values * 0.7071067811865476))


def kernel_body(sizes, *refs):
    ns, nt, nz, rows, d, sr, heads = sizes
    span = rows + 2 * WIN
    (
        a1_ref, a2_ref, g1_ref, g2_ref, meta_ref, wq_in, wo_in, gf_ref, gg_ref,
        ls_ref, sl_ref, down_ref, up_ref,
        o_x1, o_x2, o_d1, o_d2, o_down, o_up,
        wq, wo, x2s, scg, scf, na_s, pre_s, hid_s, zb_s, nf_s, proj, qb_s, kvw, pf, ob, dob_s,
        dkv, dqn, joined, hb, din, grads,
        sx, nx, nmeta,
        g_s1, g_r1, g_h, g_s2, g_r2, g_q, g_s3, g_r3, g_out,
        zs, zr, xs, xr, hs, hr, ps, pr, lsem,
        halo_s, halo_r, sec_s, sec_r, ar_s, ar_r,
    ) = refs
    s = lax.axis_index("section")
    t = lax.axis_index("tok")
    c = lax.rem(t, 2)
    z = lax.rem(t // 2, nz)
    x = t // (2 * nz)
    nchip = 2 * nz

    def tok_of(xx, zz, cc):
        return (xx * nz + zz) * 2 + cc

    partner = tok_of(x, z, 1 - c)
    xp, xm, xo = lax.rem(x + 1, NX), lax.rem(x + NX - 1, NX), lax.rem(x + 2, NX)
    right, left = lax.rem(t + 1, nt), lax.rem(t + nt - 1, nt)
    s_next, s_prev = lax.rem(s + 1, ns), lax.rem(s + ns - 1, ns)

    barrier = pltpu.get_barrier_semaphore()
    greet = [partner, left, right]
    greet += [tok_of(lax.rem(x + k, NX), z, c) for k in range(1, NX)]
    greet += [tok_of(x, lax.rem(z + k, nz), c) for k in range(1, nz)]
    for other in greet:
        pl.semaphore_signal(barrier, inc=1, device_id={"tok": other}, device_id_type=MESH)
    for other in (s_next, s_prev):
        pl.semaphore_signal(barrier, inc=1, device_id={"section": other}, device_id_type=MESH)
    pl.semaphore_wait(barrier, len(greet) + 2)

    waits = []

    def send(src, dst, ssem, rsem, where, cond=None):
        copy = pltpu.make_async_remote_copy(
            src_ref=src, dst_ref=dst, send_sem=ssem, recv_sem=rsem,
            device_id=where, device_id_type=MESH,
        )
        if cond is None:
            copy.start()
        else:
            pl.when(cond)(copy.start)
        waits.append((copy, cond))

    def arrived(dst, rsem):
        pltpu.make_async_remote_copy(
            src_ref=dst, dst_ref=dst, send_sem=rsem, recv_sem=rsem,
            device_id={"tok": partner}, device_id_type=MESH,
        ).wait_recv()

    shard = d // nt
    half = shard // 2
    flows = [(z, None, 0, 0)]
    for k in range(1, nz):
        flows.append((z - k, z - k >= 0, 1, k))
    for k in range(1, nz):
        flows.append((z + k, z + k <= nz - 1, -1, k))
    nf_ = len(flows)

    def place(w, xx, zz, part=None):
        base = tok_of(xx, zz, c) * shard
        if part is None:
            return w.at[pl.ds(pl.multiple_of(base, shard), shard)]
        return w.at[pl.ds(pl.multiple_of(base + part * half, half), half)]

    def place_of(w, xx, zz, cc, part=None):
        base = tok_of(xx, zz, cc) * shard
        if part is None:
            return w.at[pl.ds(pl.multiple_of(base, shard), shard)]
        return w.at[pl.ds(pl.multiple_of(base + part * half, half), half)]

    def spread(i, w, src, f, zf, cond):
        dst = place(w, x, zf)
        send(src, dst, xs.at[i, 0, f], xr.at[i, 0, f], {"tok": tok_of(xp, z, c)}, cond)
        send(src, dst, xs.at[i, 1, f], xr.at[i, 1, f], {"tok": tok_of(xm, z, c)}, cond)
        send(src, dst, ps.at[i, 0, f], pr.at[i, 0, f], {"tok": partner}, cond)

    def both(one, two):
        return two if one is None else jnp.logical_and(one, two)

    def own_start(i, w, w_in):
        dst = place(w, x, z)
        local = pltpu.make_async_copy(w_in, dst, lsem.at[i])
        up_ok, dn_ok = z < nz - 1, z > 0
        if nz > 1:
            send(w_in, dst, zs.at[i, 0, 0], zr.at[i, 0, 1], {"tok": tok_of(x, jnp.minimum(z + 1, nz - 1), c)}, up_ok)
            send(w_in, dst, zs.at[i, 1, 0], zr.at[i, 1, 1], {"tok": tok_of(x, jnp.maximum(z - 1, 0), c)}, dn_ok)
        spread(i, w, w_in, 0, z, None)
        local.start()
        return local

    def z_step(i, w, k):
        for way, (f, off) in enumerate(((k, -k), (nz - 1 + k, k))):
            zf, cond = flows[f][0], flows[f][1]

            def clip(v):
                return jnp.clip(v, 0, nz - 1)

            zc = clip(zf)
            dst = place(w, x, zc)
            pl.when(cond)(functools.partial(arrived, dst, zr.at[i, way, k]))
            if k < nz - 1:
                if way == 0:
                    send(dst, dst, zs.at[i, 0, k], zr.at[i, 0, k + 1], {"tok": tok_of(x, clip(z + 1), c)},
                         jnp.logical_and(cond, z < nz - 1))
                else:
                    send(dst, dst, zs.at[i, 1, k], zr.at[i, 1, k + 1], {"tok": tok_of(x, clip(z - 1), c)},
                         jnp.logical_and(cond, z > 0))
            spread(i, w, dst, f, zc, cond)

    def each_flow():
        for f in range(nf_):
            zf, cond = flows[f][0], flows[f][1]
            yield f, jnp.clip(zf, 0, nz - 1), cond

    def guarded(cond, fn):
        if cond is None:
            fn()
        else:
            pl.when(cond)(fn)

    def x_forward(i, w):
        for f, zf, cond in each_flow():
            for way, (origin, onward) in enumerate(((xm, xp), (xp, xm))):
                dst = place(w, origin, zf)
                guarded(cond, functools.partial(arrived, dst, xr.at[i, way, f]))
                piece = place(w, origin, zf, way)
                send(piece, piece, hs.at[i, way, f], hr.at[i, way, f], {"tok": tok_of(onward, z, c)}, cond)
                send(dst, dst, ps.at[i, 1 + way, f], pr.at[i, 1 + way, f], {"tok": partner}, cond)

    def halves(i, w):
        for f, zf, cond in each_flow():
            for way in range(2):
                piece = place(w, xo, zf, way)
                guarded(cond, functools.partial(arrived, piece, hr.at[i, way, f]))
                send(piece, piece, ps.at[i, 3 + way, f], pr.at[i, 3 + way, f], {"tok": partner}, cond)

    def from_partner(i, w, kind):
        for f, zf, cond in each_flow():
            origin = (x, xm, xp, xo, xo)[kind]
            dst = place_of(w, origin, zf, 1 - c, kind - 3 if kind >= 3 else None)
            guarded(cond, functools.partial(arrived, dst, pr.at[i, kind, f]))

    gain_f, gain_g = gf_ref[...], gg_ref[...]

    def tables(meta):
        row_block = lax.broadcasted_iota(jnp.int32, (rows, 128), 0) // BLOCK + t * (rows // BLOCK)
        pick = (lax.broadcasted_iota(jnp.int32, (rows, 128), 1) == row_block).astype(BF16)
        per_row = dot_last(pick, meta.astype(BF16))
        sensor, spot = per_row[:, 0:1], per_row[:, 1:2]
        first = t * (rows // BLOCK) - WIN // BLOCK
        key_block = lax.broadcasted_iota(jnp.int32, (128, span), 1) // BLOCK + first
        pick_key = (lax.broadcasted_iota(jnp.int32, (128, span), 0) == key_block).astype(BF16)
        key_spot = dot(meta.astype(BF16), pick_key)[1:2, :]
        owner = (lax.broadcasted_iota(jnp.int32, (rows, sr), 1) // RANK).astype(F32)
        mask = (owner == sensor).astype(F32)
        distance = jnp.log(1.0 + jnp.abs(spot - key_spot))
        return mask, distance

    q_idx = lax.broadcasted_iota(jnp.int32, (rows, span), 0)
    k_idx = lax.broadcasted_iota(jnp.int32, (rows, span), 1)
    key_at = k_idx + (t * rows - WIN)
    allowed = (
        (k_idx >= q_idx) & (k_idx <= q_idx + 2 * WIN) & (key_at >= 0) & (key_at < nt * rows)
    ).astype(F32)

    def adapter_forward(p, top, bottom, mask):
        scaled, inverse = layer_norm(top)
        scg[p] = scaled
        adapt_in = (scaled * gain_g).astype(BF16)
        na_s[p] = adapt_in
        pre = dot(adapt_in, down_ref[...]) * mask
        pre_s[p] = pre
        hidden = (pre * phi(pre)).astype(BF16)
        hid_s[p] = hidden
        x2s[p] = bottom - dot(hidden, up_ref[...])
        return inverse

    def adapter_backward(p, top_cot, bottom_cot, mask, inverse):
        pre = pre_s[p]
        slope = phi(pre) + pre * jnp.exp(-0.5 * pre * pre) * 0.3989422804014327
        cot = dot_last(bottom_cot, up_ref[...])
        hidden_grad = (mask * slope * cot).astype(BF16)
        grad_down = dot_first(na_s[p], hidden_grad)
        grad_up = dot_first(hid_s[p], bottom_cot)
        if p == 0:
            grads[0] = grad_down
        else:
            grads[0] = grads[0] + grad_down
        for b in range(d // sr):
            part = grad_up[:, b * sr : (b + 1) * sr]
            at = slice(b * sr, (b + 1) * sr)
            grads[1, at] = part if p == 0 else grads[1, at] + part
        back = dot_last(hidden_grad, down_ref[...])
        zb_s[p] = (top_cot + norm_back(back, gain_g, scg[p], inverse)).astype(BF16)

    def attention_norm(p):
        scaled, inverse = layer_norm(x2s[p])
        scf[p] = scaled
        nf_s[p] = (scaled * gain_f).astype(BF16)
        return inverse

    kblock = d // NX

    def qkv_block(p, xx, first):
        at = pl.ds(pl.multiple_of(xx * kblock, kblock), kblock)
        part_in = nf_s[p, :, at]
        for n in range(3):
            cols = slice(n * d, (n + 1) * d)
            part = dot(part_in, wq[at, cols])
            proj[p, :, cols] = part if first else proj[p, :, cols] + part

    def qkv_whole(p, n):
        cols = slice(n * d, (n + 1) * d)
        proj[p, :, cols] = dot(nf_s[p], wq[:, cols])

    def unit(values):
        scale = lax.rsqrt(jnp.mean(values * values, axis=-1, keepdims=True) + 1e-06)
        return values * scale, scale

    def head(h, part=0):
        return slice(part * d + h * HS, part * d + (h + 1) * HS)

    def keys_values(p):
        for h in range(heads):
            kvw[p, WIN : WIN + rows, head(h)] = unit(proj[p, :, head(h, 1)])[0].astype(BF16)
            kvw[p, WIN : WIN + rows, head(h, 1)] = proj[p, :, head(h, 2)].astype(BF16)
        first = kvw.at[p, pl.ds(WIN, WIN)]
        last = kvw.at[p, pl.ds(rows, WIN)]
        send(first, kvw.at[p, pl.ds(rows + WIN, WIN)], halo_s.at[p, 0], halo_r.at[p, 0], {"tok": left})
        send(last, kvw.at[p, pl.ds(0, WIN)], halo_s.at[p, 1], halo_r.at[p, 1], {"tok": right})

    def halo_wait(p):
        arrived(kvw.at[p, pl.ds(rows + WIN, WIN)], halo_r.at[p, 0])
        arrived(kvw.at[p, pl.ds(0, WIN)], halo_r.at[p, 1])

    def queries(p):
        for h in range(heads):
            qb_s[p, :, head(h)] = unit(proj[p, :, head(h)])[0].astype(BF16)

    def attend(p, distance):
        for h in range(heads):
            score = dot_last(qb_s[p, :, head(h)], kvw[p, :, head(h)])
            score = score * (ls_ref[0, h] / HS) - sl_ref[0, h] * distance
            weights = jnp.exp(score) * allowed
            attention = weights / jnp.sum(weights, axis=-1, keepdims=True)
            pf[p, h] = attention
            ob[p, :, head(h)] = dot(attention.astype(BF16), kvw[p, :, head(h, 1)]).astype(BF16)

    def attend_back(p):
        dob_s[p] = dot_last(zb_s[p], wo[...]).astype(BF16)
        for h in range(heads):
            mixed = dob_s[p, :, head(h)]
            attention = pf[p, h]
            value_cot = dot_last(mixed, kvw[p, :, head(h, 1)])
            centre = jnp.sum(attention * value_cot, axis=-1, keepdims=True)
            score_grad = (attention * (value_cot - centre) * (ls_ref[0, h] / HS)).astype(BF16)
            dqn[p, :, head(h)] = dot(score_grad, kvw[p, :, head(h)])
            key_grad = dot_first(score_grad, qb_s[p, :, head(h)])
            value_grad = dot_first(attention.astype(BF16), mixed)
            for part, grad in ((0, key_grad), (1, value_grad)):
                hb[p, 0:WIN, head(h, part)] = grad[0:WIN].astype(BF16)
                hb[p, WIN : 2 * WIN, head(h, part)] = grad[rows + WIN :].astype(BF16)
                dkv[p, :, head(h, part)] = grad[WIN : WIN + rows]
        send(hb.at[p, pl.ds(0, WIN)], din.at[p, pl.ds(rows - WIN, WIN)], halo_s.at[p, 2], halo_r.at[p, 2], {"tok": left})
        send(hb.at[p, pl.ds(WIN, WIN)], din.at[p, pl.ds(0, WIN)], halo_s.at[p, 3], halo_r.at[p, 3], {"tok": right})

    def back_wait(p):
        arrived(din.at[p, pl.ds(rows - WIN, WIN)], halo_r.at[p, 2])
        arrived(din.at[p, pl.ds(0, WIN)], halo_r.at[p, 3])

    def unit_back(grad, values):
        one, scale = unit(values)
        return scale * (grad - one * jnp.mean(grad * one, axis=-1, keepdims=True))

    def project_back(p, bottom_cot, inverse):
        for h in range(heads):
            joined[:, head(h)] = unit_back(dqn[p, :, head(h)], proj[p, :, head(h)]).astype(BF16)
            key_grad = dkv[p, :, head(h)] + din[p, :, head(h)].astype(F32)
            joined[:, head(h, 1)] = unit_back(key_grad, proj[p, :, head(h, 1)]).astype(BF16)
            joined[:, head(h, 2)] = (dkv[p, :, head(h, 1)] + din[p, :, head(h, 1)].astype(F32)).astype(BF16)
        back = dot_last(joined[...], wq[...])
        return bottom_cot + norm_back(back, gain_f, scf[p], inverse)

    def pass_on(k):
        send(sx.at[k], nx.at[k], sec_s.at[k], sec_r.at[k], {"section": s_prev})

    locals_ = [own_start(0, wq, wq_in)]
    mask1, dist1 = tables(meta_ref[...])
    inv_g1 = adapter_forward(0, a1_ref[...], a2_ref[...], mask1)
    sx[1] = x2s[0].astype(BF16)
    inv_f1 = attention_norm(0)
    for k in range(1, nz):
        z_step(0, wq, k)
    adapter_backward(0, g1_ref[...].astype(F32), g2_ref[...], mask1, inv_g1)
    sx[2] = zb_s[0]
    locals_.append(own_start(1, wo, wo_in))
    send(meta_ref, nmeta, sec_s.at[4], sec_r.at[4], {"section": s_prev})
    x_forward(0, wq)
    locals_[0].wait()
    from_partner(0, wq, 0)
    qkv_block(0, x, True)
    for k in range(1, nz):
        z_step(1, wo, k)
    from_partner(0, wq, 1)
    qkv_block(0, xm, False)
    from_partner(0, wq, 2)
    qkv_block(0, xp, False)
    halves(0, wq)
    pass_on(1)
    pass_on(2)
    x_forward(1, wo)
    from_partner(0, wq, 3)
    from_partner(0, wq, 4)
    qkv_block(0, xo, False)
    keys_values(0)
    queries(0)
    halves(1, wo)
    halo_wait(0)
    attend(0, dist1)
    locals_[1].wait()
    for kind in range(5):
        from_partner(1, wo, kind)
    sx[0] = (a1_ref[...] - dot(ob[0], wo[...])).astype(BF16)
    pass_on(0)
    attend_back(0)

    flag = (s < ns - 1).astype(F32)
    arrived(nmeta, sec_r.at[4])
    arrived(nx.at[1], sec_r.at[1])
    arrived(nx.at[0], sec_r.at[0])
    mask2, dist2 = tables(nmeta[...] * flag)
    top2 = nx[0].astype(F32) * flag
    inv_g2 = adapter_forward(1, top2, nx[1].astype(F32) * flag, mask2)
    o_x2[...] = x2s[1]
    inv_f2 = attention_norm(1)
    qkv_whole(1, 1)
    qkv_whole(1, 2)
    keys_values(1)

    back_wait(0)
    sx[3] = project_back(0, g2_ref[...].astype(F32), inv_f1).astype(BF16)
    pass_on(3)

    qkv_whole(1, 0)
    queries(1)
    halo_wait(1)
    attend(1, dist2)
    o_x1[...] = top2 - dot(ob[1], wo[...])

    arrived(nx.at[2], sec_r.at[2])
    arrived(nx.at[3], sec_r.at[3])
    cot2 = nx[3] * flag.astype(BF16)
    adapter_backward(1, nx[2].astype(F32) * flag, cot2, mask2, inv_g2)
    o_d1[...] = zb_s[1]

    g_s1[...] = grads[1 - c].astype(BF16)
    send(g_s1, g_r1, ar_s.at[0], ar_r.at[0], {"tok": partner})
    xrows = d // NX
    zrows = xrows // nz

    def xpart(k):
        return pl.ds(pl.multiple_of(k * xrows, xrows), xrows)

    def zpart(k):
        return pl.ds(pl.multiple_of(k * zrows, zrows), zrows)

    def fpart(xx, zz):
        return pl.ds(pl.multiple_of(xx * xrows + zz * zrows, zrows), zrows)

    attend_back(1)

    arrived(g_r1, ar_r.at[0])
    g_h[...] = grads[c] + g_r1[...].astype(F32)
    g_s2[...] = g_h[...].astype(BF16)
    for k in range(1, NX):
        to = lax.rem(x + k, NX)
        send(g_s2.at[xpart(to)], g_r2.at[k - 1], ar_s.at[k], ar_r.at[k], {"tok": tok_of(to, z, c)})

    back_wait(1)

    for k in range(1, NX):
        arrived(g_r2.at[k - 1], ar_r.at[k])
    total = g_h[xpart(x)]
    for k in range(1, NX):
        total = total + g_r2[k - 1].astype(F32)
    g_q[...] = total
    g_s3[...] = total.astype(BF16)
    for k in range(1, nz):
        to = lax.rem(z + k, nz)
        send(g_s3.at[zpart(to)], g_r3.at[k - 1], ar_s.at[NX - 1 + k], ar_r.at[NX - 1 + k], {"tok": tok_of(x, to, c)})

    o_d2[...] = project_back(1, cot2.astype(F32), inv_f2).astype(BF16)

    base = NX - 1 + nz
    for k in range(1, nz):
        arrived(g_r3.at[k - 1], ar_r.at[NX - 1 + k])
    total = g_q[zpart(z)]
    for k in range(1, nz):
        total = total + g_r3[k - 1].astype(F32)
    g_out[c, fpart(x, z)] = total.astype(BF16)
    for k in range(1, nz):
        to = lax.rem(z + k, nz)
        mine = g_out.at[c, fpart(x, z)]
        send(mine, mine, ar_s.at[base + k - 1], ar_r.at[base + k - 1], {"tok": tok_of(x, to, c)})
    for k in range(1, nz):
        came = lax.rem(z + nz - k, nz)
        arrived(g_out.at[c, fpart(x, came)], ar_r.at[base + k - 1])
    base = base + nz - 1
    for k in range(1, NX):
        to = lax.rem(x + k, NX)
        mine = g_out.at[c, xpart(x)]
        send(mine, mine, ar_s.at[base + k - 1], ar_r.at[base + k - 1], {"tok": tok_of(to, z, c)})
    for k in range(1, NX):
        came = lax.rem(x + NX - k, NX)
        arrived(g_out.at[c, xpart(came)], ar_r.at[base + k - 1])
    base = base + NX - 1
    send(g_out.at[c], g_out.at[c], ar_s.at[base], ar_r.at[base], {"tok": partner})
    arrived(g_out.at[1 - c], ar_r.at[base])
    o_down[...] = g_out[0]
    for b in range(d // sr):
        o_up[:, b * sr : (b + 1) * sr] = g_out[1, b * sr : (b + 1) * sr]

    for copy, cond in waits:
        guarded(cond, copy.wait_send)


def on_device(
    nz,
    stream_one,
    stream_two,
    grad_one,
    grad_two,
    sensor_ids,
    block_order,
    qkv_weight,
    out_weight,
    attn_gain,
    adapt_gain,
    logit_scale,
    distance_slope,
    adapt_down,
    adapt_up,
):
    ns, nt = lax.axis_size("section"), lax.axis_size("tok")
    rows, d = stream_one.shape[1:]
    sr, heads = adapt_down.shape[2], logit_scale.shape[1]
    blocks = sensor_ids.shape[1]
    span = rows + 2 * WIN
    meta = jnp.concatenate([sensor_ids, block_order, jnp.zeros((6, blocks), jnp.int32)], axis=0)
    meta = jnp.pad(meta.astype(F32), ((0, 0), (0, 128 - blocks)))
    nflow = 2 * nz - 1
    shard_rows = d // NX
    vmem = pl.BlockSpec(memory_space=pltpu.VMEM)
    smem = pl.BlockSpec(memory_space=pltpu.SMEM)
    dma = pltpu.SemaphoreType.DMA
    nar = 1 + 2 * (NX - 1) + 2 * (nz - 1) + 1
    scratch = [
        pltpu.VMEM((d, 3 * d), BF16),
        pltpu.VMEM((d, d), BF16),
        pltpu.VMEM((2, rows, d), F32),
        pltpu.VMEM((2, rows, d), F32),
        pltpu.VMEM((2, rows, d), F32),
        pltpu.VMEM((2, rows, d), BF16),
        pltpu.VMEM((2, rows, sr), F32),
        pltpu.VMEM((2, rows, sr), BF16),
        pltpu.VMEM((2, rows, d), BF16),
        pltpu.VMEM((2, rows, d), BF16),
        pltpu.VMEM((2, rows, 3 * d), F32),
        pltpu.VMEM((2, rows, d), BF16),
        pltpu.VMEM((2, span, 2 * d), BF16),
        pltpu.VMEM((2, heads, rows, span), F32),
        pltpu.VMEM((2, rows, d), BF16),
        pltpu.VMEM((2, rows, d), BF16),
        pltpu.VMEM((2, rows, 2 * d), F32),
        pltpu.VMEM((2, rows, d), F32),
        pltpu.VMEM((rows, 3 * d), BF16),
        pltpu.VMEM((2, 2 * WIN, 2 * d), BF16),
        pltpu.VMEM((2, rows, 2 * d), BF16),
        pltpu.VMEM((2, d, sr), F32),
        pltpu.VMEM((4, rows, d), BF16),
        pltpu.VMEM((4, rows, d), BF16),
        pltpu.VMEM((8, 128), F32),
        pltpu.VMEM((d, sr), BF16),
        pltpu.VMEM((d, sr), BF16),
        pltpu.VMEM((d, sr), F32),
        pltpu.VMEM((d, sr), BF16),
        pltpu.VMEM((NX - 1, shard_rows, sr), BF16),
        pltpu.VMEM((shard_rows, sr), F32),
        pltpu.VMEM((shard_rows, sr), BF16),
        pltpu.VMEM((nz - 1, shard_rows // nz, sr), BF16),
        pltpu.VMEM((2, d, sr), BF16),
        dma((2, 2, nz)),
        dma((2, 2, nz)),
        dma((2, 2, nflow)),
        dma((2, 2, nflow)),
        dma((2, 2, nflow)),
        dma((2, 2, nflow)),
        dma((2, 5, nflow)),
        dma((2, 5, nflow)),
        dma((2,)),
        dma((2, 4)),
        dma((2, 4)),
        dma((5,)),
        dma((5,)),
        dma((nar,)),
        dma((nar,)),
    ]
    outs = pl.pallas_call(
        functools.partial(kernel_body, (ns, nt, nz, rows, d, sr, heads)),
        out_shape=(
            jax.ShapeDtypeStruct((rows, d), F32),
            jax.ShapeDtypeStruct((rows, d), F32),
            jax.ShapeDtypeStruct((rows, d), BF16),
            jax.ShapeDtypeStruct((rows, d), BF16),
            jax.ShapeDtypeStruct((d, sr), BF16),
            jax.ShapeDtypeStruct((sr, d), BF16),
        ),
        in_specs=[vmem] * 9 + [smem] * 2 + [vmem] * 2,
        out_specs=[vmem] * 6,
        scratch_shapes=scratch,
        compiler_params=pltpu.CompilerParams(
            collective_id=0, has_side_effects=True, vmem_limit_bytes=48 << 20
        ),
    )(
        stream_one[0],
        stream_two[0],
        grad_one[0],
        grad_two[0],
        meta,
        qkv_weight[0],
        out_weight[0],
        attn_gain,
        adapt_gain,
        logit_scale,
        distance_slope,
        adapt_down[0],
        adapt_up[0],
    )
    return tuple(out[None] for out in outs)


def solution(mesh):
    three, two = P("section", "tok", None), P("section", None)
    whole = P("section", None, None)
    in_specs = (three,) * 4 + (two,) * 2 + (three,) * 2 + (two,) * 4 + (whole,) * 2
    out_specs = (three,) * 4 + (whole,) * 2
    nz = mesh.shape["tok"] // (2 * NX)
    return jax.shard_map(
        functools.partial(on_device, nz),
        mesh=mesh,
        in_specs=in_specs,
        out_specs=out_specs,
        check_vma=False,
    )
```

```python
import contextlib
import functools

import jax
import jax.numpy as jnp
from jax import lax
from jax.experimental import pallas as pl
from jax.experimental.pallas import tpu as pltpu
from jax.sharding import PartitionSpec as P

RANK = 16
BLOCK = 16
WIN = 32
HS = 128
NX = 4
MESH = pl.DeviceIdType.MESH
F32 = jnp.float32
BF16 = jnp.bfloat16


def stage(name):
    return contextlib.nullcontext()


def dot(left, right):
    return jnp.dot(left, right, preferred_element_type=F32)


def dot_last(left, right):
    return lax.dot_general(left, right, (((1,), (1,)), ((), ())), preferred_element_type=F32)


def dot_first(left, right):
    return lax.dot_general(left, right, (((0,), (0,)), ((), ())), preferred_element_type=F32)


def layer_norm(values):
    centred = values - jnp.mean(values, axis=-1, keepdims=True)
    inverse = lax.rsqrt(jnp.mean(centred * centred, axis=-1, keepdims=True) + 1e-05)
    return centred * inverse, inverse


def norm_back(upstream, gain, scaled, inverse):
    inner = upstream * gain
    mean_one = jnp.mean(inner, axis=-1, keepdims=True)
    mean_two = jnp.mean(inner * scaled, axis=-1, keepdims=True)
    return inverse * (inner - mean_one - scaled * mean_two)


def phi(values):
    return 0.5 * (1.0 + lax.erf(values * 0.7071067811865476))


def kernel_body(sizes, *refs):
    ns, nt, nz, rows, d, sr, heads = sizes
    span = rows + 2 * WIN
    (
        a1_in, a2_in, g1_in, g2_in, ids_in, order_in, wq_in, wo_in, gf_in, gg_in,
        ls_in, sl_in, down_in, up_in,
        o_x1, o_x2, o_d1, o_d2, o_down, o_up,
        wq, wo, x2s, scg, scf, na_s, pre_s, hid_s, zb_s, nf_s, nfw, projq, projkv, qb_s, kvw, pf, ob, dob_s,
        dkv, dqn, joined, hb, din, grads,
        sx, nx, nmeta,
        g_s1, g_r1, g_h, g_s2, g_r2, g_q, g_s3, g_r3, g_out,
        zs, zr, xs, xr, hs, hr, ps, pr, lsem,
        halo_s, halo_r, sec_s, sec_r, ar_s, ar_r,
        a1_ref, a2_ref, g1_ref, g2_ref, ids_v, order_v, gf_ref, gg_ref, down_ref, up_ref,
        meta_s, x1_v, d2_v, up_v, ls_ref, sl_ref, load_sem, store_sem,
    ) = refs
    moves = (
        (a1_in, a1_ref), (ids_in, ids_v), (order_in, order_v), (gg_in, gg_ref), (down_in, down_ref), (up_in, up_ref),
        (a2_in, a2_ref), (gf_in, gf_ref), (g1_in, g1_ref), (g2_in, g2_ref), (ls_in, ls_ref), (sl_in, sl_ref),
    )
    loads = [pltpu.make_async_copy(a, b, load_sem.at[i]) for i, (a, b) in enumerate(moves)]
    stores = []

    def store(src, dst, i):
        copy = pltpu.make_async_copy(src, dst, store_sem.at[i])
        copy.start()
        stores.append(copy)

    s = lax.axis_index("section")
    t = lax.axis_index("tok")
    c = lax.rem(t, 2)
    z = lax.rem(t // 2, nz)
    x = t // (2 * nz)
    nchip = 2 * nz

    def tok_of(xx, zz, cc):
        return (xx * nz + zz) * 2 + cc

    partner = tok_of(x, z, 1 - c)
    xp, xm, xo = lax.rem(x + 1, NX), lax.rem(x + NX - 1, NX), lax.rem(x + 2, NX)
    right, left = lax.rem(t + 1, nt), lax.rem(t + nt - 1, nt)
    s_next, s_prev = lax.rem(s + 1, ns), lax.rem(s + ns - 1, ns)

    barrier = pltpu.get_barrier_semaphore()
    greet = [partner, left, right]
    greet += [tok_of(lax.rem(x + k, NX), z, c) for k in range(1, NX)]
    greet += [tok_of(x, lax.rem(z + k, nz), c) for k in range(1, nz)]
    for other in greet:
        pl.semaphore_signal(barrier, inc=1, device_id={"tok": other}, device_id_type=MESH)
    for other in (s_next, s_prev):
        pl.semaphore_signal(barrier, inc=1, device_id={"section": other}, device_id_type=MESH)
    pl.semaphore_wait(barrier, len(greet) + 2)

    waits = []

    def send(src, dst, ssem, rsem, where, cond=None):
        copy = pltpu.make_async_remote_copy(
            src_ref=src, dst_ref=dst, send_sem=ssem, recv_sem=rsem,
            device_id=where, device_id_type=MESH,
        )
        if cond is None:
            copy.start()
        else:
            pl.when(cond)(copy.start)
        waits.append((copy, cond))

    def arrived(dst, rsem):
        pltpu.make_async_remote_copy(
            src_ref=dst, dst_ref=dst, send_sem=rsem, recv_sem=rsem,
            device_id={"tok": partner}, device_id_type=MESH,
        ).wait_recv()

    shard = d // nt
    half = shard // 2
    flows = [(z, None, 0, 0)]
    for k in range(1, nz):
        flows.append((z - k, z - k >= 0, 1, k))
    for k in range(1, nz):
        flows.append((z + k, z + k <= nz - 1, -1, k))
    nf_ = len(flows)

    def place(w, xx, zz, part=None):
        base = tok_of(xx, zz, c) * shard
        if part is None:
            return w.at[pl.ds(pl.multiple_of(base, shard), shard)]
        return w.at[pl.ds(pl.multiple_of(base + part * half, half), half)]

    def place_of(w, xx, zz, cc, part=None):
        base = tok_of(xx, zz, cc) * shard
        if part is None:
            return w.at[pl.ds(pl.multiple_of(base, shard), shard)]
        return w.at[pl.ds(pl.multiple_of(base + part * half, half), half)]

    def spread(i, w, src, f, zf, cond):
        dst = place(w, x, zf)
        send(src, dst, xs.at[i, 0, f], xr.at[i, 0, f], {"tok": tok_of(xp, z, c)}, cond)
        send(src, dst, xs.at[i, 1, f], xr.at[i, 1, f], {"tok": tok_of(xm, z, c)}, cond)
        send(src, dst, ps.at[i, 0, f], pr.at[i, 0, f], {"tok": partner}, cond)

    def both(one, two):
        return two if one is None else jnp.logical_and(one, two)

    def clip(v):
        return jnp.clip(v, 0, nz - 1)

    def z_own(i, w, w_in):
        if nz > 1:
            dst = place(w, x, z)
            send(w_in, dst, zs.at[i, 0, 0], zr.at[i, 0, 1], {"tok": tok_of(x, clip(z + 1), c)}, z < nz - 1)
            send(w_in, dst, zs.at[i, 1, 0], zr.at[i, 1, 1], {"tok": tok_of(x, clip(z - 1), c)}, z > 0)

    def x_own(i, w, w_in):
        spread(i, w, w_in, 0, z, None)
        local = pltpu.make_async_copy(w_in, place(w, x, z), lsem.at[i])
        local.start()
        return local

    def z_step(i, w, k, onward=True):
        for way, (f, step) in enumerate(((k, 1), (nz - 1 + k, -1))):
            zf, cond = flows[f][0], flows[f][1]
            zc = clip(zf)
            dst = place(w, x, zc)
            pl.when(cond)(functools.partial(arrived, dst, zr.at[i, way, k]))
            if k < nz - 1:
                inside = z < nz - 1 if way == 0 else z > 0
                send(dst, dst, zs.at[i, way, k], zr.at[i, way, k + 1], {"tok": tok_of(x, clip(z + step), c)},
                     jnp.logical_and(cond, inside))
            if onward:
                spread(i, w, dst, f, zc, cond)

    def x_rest(i, w):
        for f, zf, cond in each_flow():
            if f > 0:
                spread(i, w, place(w, x, zf), f, zf, cond)

    def each_flow(only=None):
        for k in range(nf_):
            f = (k + 1) // 2 + (nz - 1) * (k > 0 and k % 2 == 0)
            if only is not None and (k + 1) // 2 != only:
                continue
            zf, cond = flows[f][0], flows[f][1]
            yield f, jnp.clip(zf, 0, nz - 1), cond

    def guarded(cond, fn):
        if cond is None:
            fn()
        else:
            pl.when(cond)(fn)

    def x_forward(i, w, only=None):
        for f, zf, cond in each_flow(only):
            for way, (origin, onward) in enumerate(((xm, xp), (xp, xm))):
                dst = place(w, origin, zf)
                guarded(cond, functools.partial(arrived, dst, xr.at[i, way, f]))
                piece = place(w, origin, zf, way)
                send(piece, piece, hs.at[i, way, f], hr.at[i, way, f], {"tok": tok_of(onward, z, c)}, cond)
                send(dst, dst, ps.at[i, 1 + way, f], pr.at[i, 1 + way, f], {"tok": partner}, cond)

    def halves(i, w):
        for f, zf, cond in each_flow():
            for way in range(2):
                piece = place(w, xo, zf, way)
                guarded(cond, functools.partial(arrived, piece, hr.at[i, way, f]))
                send(piece, piece, ps.at[i, 3 + way, f], pr.at[i, 3 + way, f], {"tok": partner}, cond)

    def from_partner(i, w, kind):
        for f, zf, cond in each_flow():
            origin = (x, xm, xp, xo, xo)[kind]
            dst = place_of(w, origin, zf, 1 - c, kind - 3 if kind >= 3 else None)
            guarded(cond, functools.partial(arrived, dst, pr.at[i, kind, f]))

    def tables(meta):
        row_block = lax.broadcasted_iota(jnp.int32, (rows, meta.shape[1]), 0) // BLOCK + t * (rows // BLOCK)
        pick = (lax.broadcasted_iota(jnp.int32, (rows, meta.shape[1]), 1) == row_block).astype(BF16)
        per_row = dot_last(pick, meta.astype(BF16))
        sensor, spot = per_row[:, 0:1], per_row[:, 1:2]
        first = t * (rows // BLOCK) - WIN // BLOCK
        key_block = lax.broadcasted_iota(jnp.int32, (meta.shape[1], span), 1) // BLOCK + first
        pick_key = (lax.broadcasted_iota(jnp.int32, (meta.shape[1], span), 0) == key_block).astype(BF16)
        key_spot = dot(meta.astype(BF16), pick_key)[1:2, :]
        owner = (lax.broadcasted_iota(jnp.int32, (rows, sr), 1) // RANK).astype(F32)
        mask = (owner == sensor).astype(F32)
        distance = jnp.log(1.0 + jnp.abs(spot - key_spot))
        return mask, distance

    q_idx = lax.broadcasted_iota(jnp.int32, (rows, span), 0)
    k_idx = lax.broadcasted_iota(jnp.int32, (rows, span), 1)
    key_at = k_idx + (t * rows - WIN)
    allowed = (
        (k_idx >= q_idx) & (k_idx <= q_idx + 2 * WIN) & (key_at >= 0) & (key_at < nt * rows)
    ).astype(F32)

    def adapter_forward(p, top, bottom, mask):
        scaled, inverse = layer_norm(top)
        scg[p] = scaled
        adapt_in = (scaled * gain_g).astype(BF16)
        na_s[p] = adapt_in
        pre = dot(adapt_in, down_ref[...]) * mask
        pre_s[p] = pre
        hidden = (pre * phi(pre)).astype(BF16)
        hid_s[p] = hidden
        x2s[p] = bottom - dot(hidden, up_ref[...])
        return inverse

    def adapter_backward(p, top_cot, bottom_cot, mask, inverse):
        pre = pre_s[p]
        slope = phi(pre) + pre * jnp.exp(-0.5 * pre * pre) * 0.3989422804014327
        cot = dot_last(bottom_cot, up_ref[...])
        hidden_grad = (mask * slope * cot).astype(BF16)
        grad_down = dot_first(na_s[p], hidden_grad)
        grad_up = dot_first(hid_s[p], bottom_cot)
        if p == 0:
            grads[0] = grad_down
        else:
            grads[0] = grads[0] + grad_down
        for b in range(d // sr):
            part = grad_up[:, b * sr : (b + 1) * sr]
            at = slice(b * sr, (b + 1) * sr)
            grads[1, at] = part if p == 0 else grads[1, at] + part
        back = dot_last(hidden_grad, down_ref[...])
        zb_s[p] = (top_cot + norm_back(back, gain_g, scg[p], inverse)).astype(BF16)

    def attention_norm(p):
        scaled, inverse = layer_norm(x2s[p])
        scf[p] = scaled
        if p == 0:
            nfw[WIN : WIN + rows] = (scaled * gain_f).astype(BF16)
        else:
            nf_s[...] = (scaled * gain_f).astype(BF16)
        return inverse

    kblock = d // NX

    def qkv_block(xx, first):
        at = pl.ds(pl.multiple_of(xx * kblock, kblock), kblock)
        part = dot(nfw[WIN : WIN + rows, at], wq[at, 0:d])
        projq[0] = part if first else projq[0] + part
        for n in range(2):
            cols = slice(n * d, (n + 1) * d)
            part = dot(nfw[:, at], wq[at, (n + 1) * d : (n + 2) * d])
            projkv[0, :, cols] = part if first else projkv[0, :, cols] + part

    own = slice(WIN, WIN + rows)

    def kv_whole():
        for n in range(2):
            projkv[1, own, n * d : (n + 1) * d] = dot(nf_s[...], wq[:, (n + 1) * d : (n + 2) * d])

    def q_whole():
        projq[1] = dot(nf_s[...], wq[:, 0:d])

    def unit(values):
        scale = lax.rsqrt(jnp.mean(values * values, axis=-1, keepdims=True) + 1e-06)
        return values * scale, scale

    def head(h, part=0):
        return slice(part * d + h * HS, part * d + (h + 1) * HS)

    def keys_values(p):
        at = own if p else slice(0, span)
        for h in range(heads):
            kvw[p, at, head(h)] = unit(projkv[p, at, head(h)])[0].astype(BF16)
            kvw[p, at, head(h, 1)] = projkv[p, at, head(h, 1)].astype(BF16)
        if p:
            first = kvw.at[p, pl.ds(WIN, WIN)]
            last = kvw.at[p, pl.ds(rows, WIN)]
            send(first, kvw.at[p, pl.ds(rows + WIN, WIN)], halo_s.at[p, 0], halo_r.at[p, 0], {"tok": left})
            send(last, kvw.at[p, pl.ds(0, WIN)], halo_s.at[p, 1], halo_r.at[p, 1], {"tok": right})

    def norm_halo():
        first = nfw.at[pl.ds(WIN, WIN)]
        last = nfw.at[pl.ds(rows, WIN)]
        send(first, nfw.at[pl.ds(rows + WIN, WIN)], halo_s.at[0, 0], halo_r.at[0, 0], {"tok": left})
        send(last, nfw.at[pl.ds(0, WIN)], halo_s.at[0, 1], halo_r.at[0, 1], {"tok": right})

    def norm_halo_wait():
        arrived(nfw.at[pl.ds(rows + WIN, WIN)], halo_r.at[0, 0])
        arrived(nfw.at[pl.ds(0, WIN)], halo_r.at[0, 1])

    def halo_wait(p):
        arrived(kvw.at[p, pl.ds(rows + WIN, WIN)], halo_r.at[p, 0])
        arrived(kvw.at[p, pl.ds(0, WIN)], halo_r.at[p, 1])

    def queries(p):
        for h in range(heads):
            qb_s[p, :, head(h)] = unit(projq[p, :, head(h)])[0].astype(BF16)

    def attend(p, distance):
        for h in range(heads):
            score = dot_last(qb_s[p, :, head(h)], kvw[p, :, head(h)])
            score = score * (ls_ref[0, h] / HS) - sl_ref[0, h] * distance
            weights = jnp.exp(score) * allowed
            attention = weights / jnp.sum(weights, axis=-1, keepdims=True)
            pf[p, h] = attention
            ob[p, :, head(h)] = dot(attention.astype(BF16), kvw[p, :, head(h, 1)]).astype(BF16)

    def mixed_back(p):
        dob_s[p] = dot_last(zb_s[p], wo[...]).astype(BF16)

    def attend_back(p):
        for h in range(heads):
            mixed = dob_s[p, :, head(h)]
            attention = pf[p, h]
            value_cot = dot_last(mixed, kvw[p, :, head(h, 1)])
            centre = jnp.sum(attention * value_cot, axis=-1, keepdims=True)
            score_grad = (attention * (value_cot - centre) * (ls_ref[0, h] / HS)).astype(BF16)
            dqn[p, :, head(h)] = dot(score_grad, kvw[p, :, head(h)])
            key_grad = dot_first(score_grad, qb_s[p, :, head(h)])
            value_grad = dot_first(attention.astype(BF16), mixed)
            for part, grad in ((0, key_grad), (1, value_grad)):
                hb[p, 0:WIN, head(h, part)] = grad[0:WIN].astype(BF16)
                hb[p, WIN : 2 * WIN, head(h, part)] = grad[rows + WIN :].astype(BF16)
                dkv[p, :, head(h, part)] = grad[WIN : WIN + rows]
        send(hb.at[p, pl.ds(0, WIN)], din.at[p, pl.ds(rows - WIN, WIN)], halo_s.at[p, 2], halo_r.at[p, 2], {"tok": left})
        send(hb.at[p, pl.ds(WIN, WIN)], din.at[p, pl.ds(0, WIN)], halo_s.at[p, 3], halo_r.at[p, 3], {"tok": right})

    def back_wait(p):
        arrived(din.at[p, pl.ds(rows - WIN, WIN)], halo_r.at[p, 2])
        arrived(din.at[p, pl.ds(0, WIN)], halo_r.at[p, 3])

    def unit_back(grad, values):
        one, scale = unit(values)
        return scale * (grad - one * jnp.mean(grad * one, axis=-1, keepdims=True))

    def join_back(p):
        for h in range(heads):
            joined[:, head(h)] = unit_back(dqn[p, :, head(h)], projq[p, :, head(h)]).astype(BF16)
            key_grad = dkv[p, :, head(h)] + din[p, :, head(h)].astype(F32)
            joined[:, head(h, 1)] = unit_back(key_grad, projkv[p, own, head(h)]).astype(BF16)
            joined[:, head(h, 2)] = (dkv[p, :, head(h, 1)] + din[p, :, head(h, 1)].astype(F32)).astype(BF16)

    def product_back():
        return dot_last(joined[...], wq[...])

    def project_back(p, bottom_cot, inverse):
        join_back(p)
        return bottom_cot + norm_back(product_back(), gain_f, scf[p], inverse)

    def pass_on(k):
        send(sx.at[k], nx.at[k], sec_s.at[k], sec_r.at[k], {"section": s_prev})

    with stage("start"):
        for copy in loads:
            copy.start()
        z_own(0, wq, wq_in)
        locals_ = [x_own(0, wq, wq_in)]
        z_own(1, wo, wo_in)
    with stage("load"):
        for copy in loads:
            copy.wait()
        meta_s[0:1] = ids_v[...].astype(F32)
        meta_s[1:2] = order_v[...].astype(F32)
        meta_s[2:8] = jnp.zeros((6, meta_s.shape[1]), F32)
    gain_f, gain_g = gf_ref[...], gg_ref[...]
    with stage("adapter_fwd1"):
        mask1, dist1 = tables(meta_s[...])
        inv_g1 = adapter_forward(0, a1_ref[...], a2_ref[...], mask1)
        sx[1] = x2s[0].astype(BF16)
        inv_f1 = attention_norm(0)
        norm_halo()
    with stage("adapter_bwd1"):
        adapter_backward(0, g1_ref[...].astype(F32), g2_ref[...], mask1, inv_g1)
        sx[2] = zb_s[0]
    for k in range(1, nz):
        with stage(f"zq{k}"):
            z_step(0, wq, k)
        with stage(f"zo{k}"):
            z_step(1, wo, k, False)
        with stage(f"xq{k - 1}"):
            x_forward(0, wq, k - 1)
    send(meta_s, nmeta, sec_s.at[4], sec_r.at[4], {"section": s_prev})
    pass_on(1)
    pass_on(2)
    with stage("xq_last"):
        x_forward(0, wq, nz - 1)
    locals_.append(x_own(1, wo, wo_in))
    x_rest(1, wo)
    with stage("part0"):
        locals_[0].wait()
        norm_halo_wait()
        from_partner(0, wq, 0)
    with stage("qkv_a"):
        qkv_block(x, True)
    with stage("part12"):
        from_partner(0, wq, 1)
        qkv_block(xm, False)
        from_partner(0, wq, 2)
        qkv_block(xp, False)
    with stage("halves"):
        halves(0, wq)
    with stage("part34"):
        from_partner(0, wq, 3)
        from_partner(0, wq, 4)
    with stage("qkv_b"):
        qkv_block(xo, False)
    with stage("kv1"):
        keys_values(0)
        queries(0)
    with stage("xo"):
        x_forward(1, wo)
    with stage("attend1"):
        attend(0, dist1)
    with stage("halves_o"):
        halves(1, wo)
    with stage("part_o"):
        locals_[1].wait()
        for kind in range(5):
            from_partner(1, wo, kind)
    with stage("out1"):
        sx[0] = (a1_ref[...] - dot(ob[0], wo[...])).astype(BF16)
    with stage("dob1"):
        mixed_back(0)
    with stage("attend_back1"):
        attend_back(0)
        pass_on(0)
    with stage("back_wait1"):
        back_wait(0)
    with stage("project_back1"):
        sx[3] = project_back(0, g2_ref[...].astype(F32), inv_f1).astype(BF16)
        pass_on(3)

    flag = (s < ns - 1).astype(F32)
    with stage("sec_wait"):
        arrived(nmeta, sec_r.at[4])
        arrived(nx.at[1], sec_r.at[1])
        arrived(nx.at[0], sec_r.at[0])
    with stage("adapter_fwd2"):
        mask2, dist2 = tables(nmeta[...] * flag)
        top2 = nx[0].astype(F32) * flag
        inv_g2 = adapter_forward(1, top2, nx[1].astype(F32) * flag, mask2)
        inv_f2 = attention_norm(1)
        store(x2s.at[1], o_x2, 1)
    with stage("kv2"):
        kv_whole()
        keys_values(1)
    with stage("q2"):
        q_whole()
        queries(1)
    with stage("halo2"):
        halo_wait(1)
    with stage("attend2"):
        attend(1, dist2)
    with stage("sec_wait2"):
        arrived(nx.at[2], sec_r.at[2])
        arrived(nx.at[3], sec_r.at[3])
    with stage("adapter_bwd2"):
        cot2 = nx[3] * flag.astype(BF16)
        adapter_backward(1, nx[2].astype(F32) * flag, cot2, mask2, inv_g2)
        store(zb_s.at[1], o_d1, 2)

    xrows = d // NX
    zrows = xrows // nz

    def xpart(k):
        return pl.ds(pl.multiple_of(k * xrows, xrows), xrows)

    def zpart(k):
        return pl.ds(pl.multiple_of(k * zrows, zrows), zrows)

    def fpart(xx, zz):
        return pl.ds(pl.multiple_of(xx * xrows + zz * zrows, zrows), zrows)

    with stage("ar0"):
        g_s1[...] = grads[1 - c].astype(BF16)
        send(g_s1, g_r1, ar_s.at[0], ar_r.at[0], {"tok": partner})
    with stage("dob2"):
        mixed_back(1)
    with stage("ar1"):
        arrived(g_r1, ar_r.at[0])
        g_h[...] = grads[c] + g_r1[...].astype(F32)
        g_s2[...] = g_h[...].astype(BF16)
        for k in range(1, NX):
            to = lax.rem(x + k, NX)
            send(g_s2.at[xpart(to)], g_r2.at[k - 1], ar_s.at[k], ar_r.at[k], {"tok": tok_of(to, z, c)})
    with stage("attend_back2"):
        attend_back(1)
    with stage("out2"):
        x1_v[...] = top2 - dot(ob[1], wo[...])
        store(x1_v, o_x1, 0)
    with stage("ar2"):
        for k in range(1, NX):
            arrived(g_r2.at[k - 1], ar_r.at[k])
        total = g_h[xpart(x)]
        for k in range(1, NX):
            total = total + g_r2[k - 1].astype(F32)
        g_q[...] = total
        g_s3[...] = total.astype(BF16)
        for k in range(1, nz):
            to = lax.rem(z + k, nz)
            send(g_s3.at[zpart(to)], g_r3.at[k - 1], ar_s.at[NX - 1 + k], ar_r.at[NX - 1 + k], {"tok": tok_of(x, to, c)})
    with stage("back_wait2"):
        back_wait(1)
    with stage("join2"):
        join_back(1)
    base = NX - 1 + nz
    with stage("ar3"):
        for k in range(1, nz):
            arrived(g_r3.at[k - 1], ar_r.at[NX - 1 + k])
        total = g_q[zpart(z)]
        for k in range(1, nz):
            total = total + g_r3[k - 1].astype(F32)
        g_out[c, fpart(x, z)] = total.astype(BF16)
        for k in range(1, nz):
            to = lax.rem(z + k, nz)
            mine = g_out.at[c, fpart(x, z)]
            send(mine, mine, ar_s.at[base + k - 1], ar_r.at[base + k - 1], {"tok": tok_of(x, to, c)})
    with stage("project_back2"):
        back = product_back()
    with stage("norm_back2"):
        d2_v[...] = (cot2.astype(F32) + norm_back(back, gain_f, scf[1], inv_f2)).astype(BF16)
        store(d2_v, o_d2, 3)
    with stage("ar4"):
        for k in range(1, nz):
            came = lax.rem(z + nz - k, nz)
            arrived(g_out.at[c, fpart(x, came)], ar_r.at[base + k - 1])
        base = base + nz - 1
        last = base + NX - 1
        mine = g_out.at[c, xpart(x)]
        for k in (1, 3, 2):
            to = lax.rem(x + k, NX)
            send(mine, mine, ar_s.at[base + k - 1], ar_r.at[base + k - 1], {"tok": tok_of(to, z, c)})
        send(mine, mine, ar_s.at[last], ar_r.at[last], {"tok": partner})
    with stage("ar5"):
        for k in (1, 3, 2):
            came = g_out.at[c, xpart(lax.rem(x + NX - k, NX))]
            arrived(came, ar_r.at[base + k - 1])
            send(came, came, ar_s.at[last + k], ar_r.at[last + k], {"tok": partner})
    with stage("ar6"):
        for k in range(NX):
            arrived(g_out.at[1 - c, xpart(lax.rem(x + NX - k, NX))], ar_r.at[last + k])
        store(g_out.at[0], o_down, 4)
        for b in range(d // sr):
            up_v[:, b * sr : (b + 1) * sr] = g_out[1, b * sr : (b + 1) * sr]
        store(up_v, o_up, 5)
    with stage("drain"):
        for copy, cond in waits:
            guarded(cond, copy.wait_send)
        for copy in stores:
            copy.wait()


def on_device(
    nz,
    stream_one,
    stream_two,
    grad_one,
    grad_two,
    sensor_ids,
    block_order,
    qkv_weight,
    out_weight,
    attn_gain,
    adapt_gain,
    logit_scale,
    distance_slope,
    adapt_down,
    adapt_up,
):
    ns, nt = lax.axis_size("section"), lax.axis_size("tok")
    rows, d = stream_one.shape[1:]
    sr, heads = adapt_down.shape[2], logit_scale.shape[1]
    blocks = sensor_ids.shape[1]
    span = rows + 2 * WIN
    nflow = 2 * nz - 1
    shard_rows = d // NX
    hbm = pl.BlockSpec(memory_space=pltpu.HBM)
    dma = pltpu.SemaphoreType.DMA
    nar = 1 + 2 * (NX - 1) + 2 * (nz - 1) + NX
    scratch = [
        pltpu.VMEM((d, 3 * d), BF16),
        pltpu.VMEM((d, d), BF16),
        pltpu.VMEM((2, rows, d), F32),
        pltpu.VMEM((2, rows, d), F32),
        pltpu.VMEM((2, rows, d), F32),
        pltpu.VMEM((2, rows, d), BF16),
        pltpu.VMEM((2, rows, sr), F32),
        pltpu.VMEM((2, rows, sr), BF16),
        pltpu.VMEM((2, rows, d), BF16),
        pltpu.VMEM((rows, d), BF16),
        pltpu.VMEM((span, d), BF16),
        pltpu.VMEM((2, rows, d), F32),
        pltpu.VMEM((2, span, 2 * d), F32),
        pltpu.VMEM((2, rows, d), BF16),
        pltpu.VMEM((2, span, 2 * d), BF16),
        pltpu.VMEM((2, heads, rows, span), F32),
        pltpu.VMEM((2, rows, d), BF16),
        pltpu.VMEM((2, rows, d), BF16),
        pltpu.VMEM((2, rows, 2 * d), F32),
        pltpu.VMEM((2, rows, d), F32),
        pltpu.VMEM((rows, 3 * d), BF16),
        pltpu.VMEM((2, 2 * WIN, 2 * d), BF16),
        pltpu.VMEM((2, rows, 2 * d), BF16),
        pltpu.VMEM((2, d, sr), F32),
        pltpu.VMEM((4, rows, d), BF16),
        pltpu.VMEM((4, rows, d), BF16),
        pltpu.VMEM((8, blocks), F32),
        pltpu.VMEM((d, sr), BF16),
        pltpu.VMEM((d, sr), BF16),
        pltpu.VMEM((d, sr), F32),
        pltpu.VMEM((d, sr), BF16),
        pltpu.VMEM((NX - 1, shard_rows, sr), BF16),
        pltpu.VMEM((shard_rows, sr), F32),
        pltpu.VMEM((shard_rows, sr), BF16),
        pltpu.VMEM((nz - 1, shard_rows // nz, sr), BF16),
        pltpu.VMEM((2, d, sr), BF16),
        dma((2, 2, nz)),
        dma((2, 2, nz)),
        dma((2, 2, nflow)),
        dma((2, 2, nflow)),
        dma((2, 2, nflow)),
        dma((2, 2, nflow)),
        dma((2, 5, nflow)),
        dma((2, 5, nflow)),
        dma((2,)),
        dma((2, 4)),
        dma((2, 4)),
        dma((5,)),
        dma((5,)),
        dma((nar,)),
        dma((nar,)),
        pltpu.VMEM((rows, d), F32),
        pltpu.VMEM((rows, d), F32),
        pltpu.VMEM((rows, d), BF16),
        pltpu.VMEM((rows, d), BF16),
        pltpu.VMEM((1, blocks), jnp.int32),
        pltpu.VMEM((1, blocks), jnp.int32),
        pltpu.VMEM((1, d), F32),
        pltpu.VMEM((1, d), F32),
        pltpu.VMEM((d, sr), BF16),
        pltpu.VMEM((sr, d), BF16),
        pltpu.VMEM((8, blocks), F32),
        pltpu.VMEM((rows, d), F32),
        pltpu.VMEM((rows, d), BF16),
        pltpu.VMEM((sr, d), BF16),
        pltpu.SMEM((1, heads), F32),
        pltpu.SMEM((1, heads), F32),
        dma((12,)),
        dma((6,)),
    ]
    big = (
        stream_one[0],
        stream_two[0],
        grad_one[0],
        grad_two[0],
        sensor_ids,
        block_order,
        qkv_weight[0],
        out_weight[0],
        attn_gain,
        adapt_gain,
        logit_scale,
        distance_slope,
        adapt_down[0],
        adapt_up[0],
    )
    outs = pl.pallas_call(
        functools.partial(kernel_body, (ns, nt, nz, rows, d, sr, heads)),
        out_shape=(
            jax.ShapeDtypeStruct((rows, d), F32),
            jax.ShapeDtypeStruct((rows, d), F32),
            jax.ShapeDtypeStruct((rows, d), BF16),
            jax.ShapeDtypeStruct((rows, d), BF16),
            jax.ShapeDtypeStruct((d, sr), BF16),
            jax.ShapeDtypeStruct((sr, d), BF16),
        ),
        in_specs=[hbm] * 14,
        out_specs=[hbm] * 6,
        scratch_shapes=scratch,
        compiler_params=pltpu.CompilerParams(
            collective_id=0, has_side_effects=True, vmem_limit_bytes=48 << 20
        ),
    )(
        *(pltpu.with_memory_space_constraint(arr, pltpu.HBM) for arr in big),
    )
    return tuple(out[None] for out in put_out(outs))


def put_out(values):
    def body(*refs):
        n = len(values)
        copies = [pltpu.make_async_copy(refs[i], refs[n + i], refs[2 * n].at[i]) for i in range(n)]
        for copy in copies:
            copy.start()
        for copy in copies:
            copy.wait()

    anywhere = pl.BlockSpec(memory_space=pl.ANY)
    return pl.pallas_call(
        body,
        out_shape=tuple(pltpu.HBM(v.shape, v.dtype) for v in values),
        in_specs=[anywhere] * len(values),
        out_specs=[pl.BlockSpec(memory_space=pltpu.HBM)] * len(values),
        scratch_shapes=[pltpu.SemaphoreType.DMA((len(values),))],
        compiler_params=pltpu.CompilerParams(vmem_limit_bytes=1 << 20),
    )(*values)


def solution(mesh):
    three, two = P("section", "tok", None), P("section", None)
    whole = P("section", None, None)
    in_specs = (three,) * 4 + (two,) * 2 + (three,) * 2 + (two,) * 4 + (whole,) * 2
    out_specs = (three,) * 4 + (whole,) * 2
    nz = mesh.shape["tok"] // (2 * NX)
    return jax.shard_map(
        functools.partial(on_device, nz),
        mesh=mesh,
        in_specs=in_specs,
        out_specs=out_specs,
        check_vma=False,
    )
```

```python
import contextlib
import functools

import jax
import jax.numpy as jnp
from jax import lax
from jax.experimental import pallas as pl
from jax.experimental.pallas import tpu as pltpu
from jax.sharding import PartitionSpec as P

RANK = 16
BLOCK = 16
WIN = 32
HS = 128
NX = 4
MESH = pl.DeviceIdType.MESH
F32 = jnp.float32
BF16 = jnp.bfloat16


def stage(name):
    return contextlib.nullcontext()


def dot(left, right):
    return jnp.dot(left, right, preferred_element_type=F32)


def dot_last(left, right):
    return lax.dot_general(left, right, (((1,), (1,)), ((), ())), preferred_element_type=F32)


def dot_first(left, right):
    return lax.dot_general(left, right, (((0,), (0,)), ((), ())), preferred_element_type=F32)


def layer_norm(values):
    centred = values - jnp.mean(values, axis=-1, keepdims=True)
    inverse = lax.rsqrt(jnp.mean(centred * centred, axis=-1, keepdims=True) + 1e-05)
    return centred * inverse, inverse


def norm_back(upstream, gain, scaled, inverse):
    inner = upstream * gain
    mean_one = jnp.mean(inner, axis=-1, keepdims=True)
    mean_two = jnp.mean(inner * scaled, axis=-1, keepdims=True)
    return inverse * (inner - mean_one - scaled * mean_two)


def phi(values):
    return 0.5 * (1.0 + lax.erf(values * 0.7071067811865476))


def kernel_body(sizes, *refs):
    ns, nt, nz, rows, d, sr, heads = sizes
    span = rows + 2 * WIN
    (
        a1_in, a2_in, g1_in, g2_in, ids_in, order_in, wq_in, wo_in, gf_in, gg_in,
        ls_in, sl_in, down_in, up_in,
        o_x1, o_x2, o_d1, o_d2, o_down, o_up,
        wq, wo, x2s, scg, scf, na_s, pre_s, hid_s, zb_s, nf_s, nfw, projq, projkv, qb_s, kvw, pf, ob, dob_s,
        dkv, dqn, joined, hb, din, grads,
        sx, nx, nmeta,
        g_s1, g_r1, g_h, g_s2, g_r2, g_q, g_s3, g_r3, g_out,
        zs, zr, xs, xr, hs, hr, ps, pr, lsem,
        halo_s, halo_r, sec_s, sec_r, ar_s, ar_r,
        a1_ref, a2_ref, g1_ref, g2_ref, ids_v, order_v, gf_ref, gg_ref, down_ref, up_ref,
        meta_s, x1_v, d2_v, up_v, ls_ref, sl_ref, load_sem, store_sem,
    ) = refs
    moves = (
        (a1_in, a1_ref), (ids_in, ids_v), (order_in, order_v), (gg_in, gg_ref), (down_in, down_ref), (up_in, up_ref),
        (a2_in, a2_ref), (gf_in, gf_ref), (g1_in, g1_ref), (g2_in, g2_ref), (ls_in, ls_ref), (sl_in, sl_ref),
    )
    loads = [pltpu.make_async_copy(a, b, load_sem.at[i]) for i, (a, b) in enumerate(moves)]
    stores = []

    def store(src, dst, i):
        copy = pltpu.make_async_copy(src, dst, store_sem.at[i])
        copy.start()
        stores.append(copy)

    s = lax.axis_index("section")
    t = lax.axis_index("tok")
    c = lax.rem(t, 2)
    z = lax.rem(t // 2, nz)
    x = t // (2 * nz)
    nchip = 2 * nz

    def tok_of(xx, zz, cc):
        return (xx * nz + zz) * 2 + cc

    partner = tok_of(x, z, 1 - c)
    xp, xm, xo = lax.rem(x + 1, NX), lax.rem(x + NX - 1, NX), lax.rem(x + 2, NX)
    right, left = lax.rem(t + 1, nt), lax.rem(t + nt - 1, nt)
    s_next, s_prev = lax.rem(s + 1, ns), lax.rem(s + ns - 1, ns)

    barrier = pltpu.get_barrier_semaphore()
    greet = [partner, left, right]
    greet += [tok_of(lax.rem(x + k, NX), z, c) for k in range(1, NX)]
    greet += [tok_of(x, lax.rem(z + k, nz), c) for k in range(1, nz)]
    for other in greet:
        pl.semaphore_signal(barrier, inc=1, device_id={"tok": other}, device_id_type=MESH)
    for other in (s_next, s_prev):
        pl.semaphore_signal(barrier, inc=1, device_id={"section": other}, device_id_type=MESH)
    pl.semaphore_wait(barrier, len(greet) + 2)

    waits = []

    def send(src, dst, ssem, rsem, where, cond=None):
        copy = pltpu.make_async_remote_copy(
            src_ref=src, dst_ref=dst, send_sem=ssem, recv_sem=rsem,
            device_id=where, device_id_type=MESH,
        )
        if cond is None:
            copy.start()
        else:
            pl.when(cond)(copy.start)
        waits.append((copy, cond))

    def arrived(dst, rsem):
        pltpu.make_async_remote_copy(
            src_ref=dst, dst_ref=dst, send_sem=rsem, recv_sem=rsem,
            device_id={"tok": partner}, device_id_type=MESH,
        ).wait_recv()

    shard = d // nt
    half = shard // 2
    flows = [(z, None, 0, 0)]
    for k in range(1, nz):
        flows.append((z - k, z - k >= 0, 1, k))
    for k in range(1, nz):
        flows.append((z + k, z + k <= nz - 1, -1, k))
    nf_ = len(flows)

    def place(w, xx, zz, part=None):
        base = tok_of(xx, zz, c) * shard
        if part is None:
            return w.at[pl.ds(pl.multiple_of(base, shard), shard)]
        return w.at[pl.ds(pl.multiple_of(base + part * half, half), half)]

    def place_of(w, xx, zz, cc, part=None):
        base = tok_of(xx, zz, cc) * shard
        if part is None:
            return w.at[pl.ds(pl.multiple_of(base, shard), shard)]
        return w.at[pl.ds(pl.multiple_of(base + part * half, half), half)]

    def spread(i, w, src, f, zf, cond):
        dst = place(w, x, zf)
        send(src, dst, xs.at[i, 0, f], xr.at[i, 0, f], {"tok": tok_of(xp, z, c)}, cond)
        send(src, dst, xs.at[i, 1, f], xr.at[i, 1, f], {"tok": tok_of(xm, z, c)}, cond)
        send(src, dst, ps.at[i, 0, f], pr.at[i, 0, f], {"tok": partner}, cond)

    def clip(v):
        return jnp.clip(v, 0, nz - 1)

    def z_own(i, w, w_in):
        if nz > 1:
            dst = place(w, x, z)
            send(w_in, dst, zs.at[i, 0, 0], zr.at[i, 0, 1], {"tok": tok_of(x, clip(z + 1), c)}, z < nz - 1)
            send(w_in, dst, zs.at[i, 1, 0], zr.at[i, 1, 1], {"tok": tok_of(x, clip(z - 1), c)}, z > 0)

    def x_own(i, w, w_in):
        spread(i, w, w_in, 0, z, None)
        local = pltpu.make_async_copy(w_in, place(w, x, z), lsem.at[i])
        local.start()
        return local

    def z_step(i, w, k, onward=True):
        for way, (f, step) in enumerate(((k, 1), (nz - 1 + k, -1))):
            zf, cond = flows[f][0], flows[f][1]
            zc = clip(zf)
            dst = place(w, x, zc)
            pl.when(cond)(functools.partial(arrived, dst, zr.at[i, way, k]))
            if k < nz - 1:
                inside = z < nz - 1 if way == 0 else z > 0
                send(dst, dst, zs.at[i, way, k], zr.at[i, way, k + 1], {"tok": tok_of(x, clip(z + step), c)},
                     jnp.logical_and(cond, inside))
            if onward:
                spread(i, w, dst, f, zc, cond)

    def x_rest(i, w):
        for f, zf, cond in each_flow():
            if f not in (0, 1, nz):
                spread(i, w, place(w, x, zf), f, zf, cond)

    def each_flow(only=None):
        for k in range(nf_):
            f = (k + 1) // 2 + (nz - 1) * (k > 0 and k % 2 == 0)
            if only is not None and (k + 1) // 2 != only:
                continue
            zf, cond = flows[f][0], flows[f][1]
            yield f, jnp.clip(zf, 0, nz - 1), cond

    def guarded(cond, fn):
        if cond is None:
            fn()
        else:
            pl.when(cond)(fn)

    def x_forward(i, w, only=None):
        for f, zf, cond in each_flow(only):
            for way, (origin, onward) in enumerate(((xm, xp), (xp, xm))):
                dst = place(w, origin, zf)
                guarded(cond, functools.partial(arrived, dst, xr.at[i, way, f]))
                piece = place(w, origin, zf, way)
                send(piece, piece, hs.at[i, way, f], hr.at[i, way, f], {"tok": tok_of(onward, z, c)}, cond)
                send(dst, dst, ps.at[i, 1 + way, f], pr.at[i, 1 + way, f], {"tok": partner}, cond)

    def halves(i, w):
        for f, zf, cond in each_flow():
            for way in range(2):
                piece = place(w, xo, zf, way)
                guarded(cond, functools.partial(arrived, piece, hr.at[i, way, f]))
                send(piece, piece, ps.at[i, 3 + way, f], pr.at[i, 3 + way, f], {"tok": partner}, cond)

    def from_partner(i, w, kind):
        for f, zf, cond in each_flow():
            origin = (x, xm, xp, xo, xo)[kind]
            dst = place_of(w, origin, zf, 1 - c, kind - 3 if kind >= 3 else None)
            guarded(cond, functools.partial(arrived, dst, pr.at[i, kind, f]))

    def tables(meta):
        row_block = lax.broadcasted_iota(jnp.int32, (rows, meta.shape[1]), 0) // BLOCK + t * (rows // BLOCK)
        pick = (lax.broadcasted_iota(jnp.int32, (rows, meta.shape[1]), 1) == row_block).astype(BF16)
        per_row = dot_last(pick, meta.astype(BF16))
        sensor, spot = per_row[:, 0:1], per_row[:, 1:2]
        first = t * (rows // BLOCK) - WIN // BLOCK
        key_block = lax.broadcasted_iota(jnp.int32, (meta.shape[1], span), 1) // BLOCK + first
        pick_key = (lax.broadcasted_iota(jnp.int32, (meta.shape[1], span), 0) == key_block).astype(BF16)
        key_spot = dot(meta.astype(BF16), pick_key)[1:2, :]
        owner = (lax.broadcasted_iota(jnp.int32, (rows, sr), 1) // RANK).astype(F32)
        mask = (owner == sensor).astype(F32)
        distance = jnp.log(1.0 + jnp.abs(spot - key_spot))
        return mask, distance

    q_idx = lax.broadcasted_iota(jnp.int32, (rows, span), 0)
    k_idx = lax.broadcasted_iota(jnp.int32, (rows, span), 1)
    key_at = k_idx + (t * rows - WIN)
    allowed = (
        (k_idx >= q_idx) & (k_idx <= q_idx + 2 * WIN) & (key_at >= 0) & (key_at < nt * rows)
    ).astype(F32)

    def adapter_forward(p, top, bottom, mask):
        scaled, inverse = layer_norm(top)
        scg[p] = scaled
        adapt_in = (scaled * gain_g).astype(BF16)
        na_s[p] = adapt_in
        pre = dot(adapt_in, down_ref[...]) * mask
        pre_s[p] = pre
        hidden = (pre * phi(pre)).astype(BF16)
        hid_s[p] = hidden
        x2s[p] = bottom - dot(hidden, up_ref[...])
        return inverse

    def adapter_backward(p, top_cot, bottom_cot, mask, inverse):
        pre = pre_s[p]
        slope = phi(pre) + pre * jnp.exp(-0.5 * pre * pre) * 0.3989422804014327
        cot = dot_last(bottom_cot, up_ref[...])
        hidden_grad = (mask * slope * cot).astype(BF16)
        grad_down = dot_first(na_s[p], hidden_grad)
        grad_up = dot_first(hid_s[p], bottom_cot)
        if p == 0:
            grads[0] = grad_down
        else:
            grads[0] = grads[0] + grad_down
        for b in range(d // sr):
            part = grad_up[:, b * sr : (b + 1) * sr]
            at = slice(b * sr, (b + 1) * sr)
            grads[1, at] = part if p == 0 else grads[1, at] + part
        back = dot_last(hidden_grad, down_ref[...])
        zb_s[p] = (top_cot + norm_back(back, gain_g, scg[p], inverse)).astype(BF16)

    def attention_norm(p):
        scaled, inverse = layer_norm(x2s[p])
        scf[p] = scaled
        if p == 0:
            nfw[WIN : WIN + rows] = (scaled * gain_f).astype(BF16)
        else:
            nf_s[...] = (scaled * gain_f).astype(BF16)
        return inverse

    kblock = d // NX

    def qkv_block(xx, first):
        at = pl.ds(pl.multiple_of(xx * kblock, kblock), kblock)
        part = dot(nfw[WIN : WIN + rows, at], wq[at, 0:d])
        projq[0] = part if first else projq[0] + part
        for n in range(2):
            cols = slice(n * d, (n + 1) * d)
            part = dot(nfw[:, at], wq[at, (n + 1) * d : (n + 2) * d])
            projkv[0, :, cols] = part if first else projkv[0, :, cols] + part

    own = slice(WIN, WIN + rows)

    def kv_whole():
        for n in range(2):
            projkv[1, own, n * d : (n + 1) * d] = dot(nf_s[...], wq[:, (n + 1) * d : (n + 2) * d])

    def q_whole():
        projq[1] = dot(nf_s[...], wq[:, 0:d])

    def unit(values):
        scale = lax.rsqrt(jnp.mean(values * values, axis=-1, keepdims=True) + 1e-06)
        return values * scale, scale

    def head(h, part=0):
        return slice(part * d + h * HS, part * d + (h + 1) * HS)

    def keys_values(p):
        at = own if p else slice(0, span)
        for h in range(heads):
            kvw[p, at, head(h)] = unit(projkv[p, at, head(h)])[0].astype(BF16)
            kvw[p, at, head(h, 1)] = projkv[p, at, head(h, 1)].astype(BF16)
        if p:
            first = kvw.at[p, pl.ds(WIN, WIN)]
            last = kvw.at[p, pl.ds(rows, WIN)]
            send(first, kvw.at[p, pl.ds(rows + WIN, WIN)], halo_s.at[p, 0], halo_r.at[p, 0], {"tok": left})
            send(last, kvw.at[p, pl.ds(0, WIN)], halo_s.at[p, 1], halo_r.at[p, 1], {"tok": right})

    def norm_halo():
        first = nfw.at[pl.ds(WIN, WIN)]
        last = nfw.at[pl.ds(rows, WIN)]
        send(first, nfw.at[pl.ds(rows + WIN, WIN)], halo_s.at[0, 0], halo_r.at[0, 0], {"tok": left})
        send(last, nfw.at[pl.ds(0, WIN)], halo_s.at[0, 1], halo_r.at[0, 1], {"tok": right})

    def norm_halo_wait():
        arrived(nfw.at[pl.ds(rows + WIN, WIN)], halo_r.at[0, 0])
        arrived(nfw.at[pl.ds(0, WIN)], halo_r.at[0, 1])

    def halo_wait(p):
        arrived(kvw.at[p, pl.ds(rows + WIN, WIN)], halo_r.at[p, 0])
        arrived(kvw.at[p, pl.ds(0, WIN)], halo_r.at[p, 1])

    def queries(p):
        for h in range(heads):
            qb_s[p, :, head(h)] = unit(projq[p, :, head(h)])[0].astype(BF16)

    def attend(p, distance):
        for h in range(heads):
            score = dot_last(qb_s[p, :, head(h)], kvw[p, :, head(h)])
            score = score * (ls_ref[0, h] / HS) - sl_ref[0, h] * distance
            weights = jnp.exp(score) * allowed
            attention = weights / jnp.sum(weights, axis=-1, keepdims=True)
            pf[p, h] = attention
            ob[p, :, head(h)] = dot(attention.astype(BF16), kvw[p, :, head(h, 1)]).astype(BF16)

    def mixed_back(p):
        dob_s[p] = dot_last(zb_s[p], wo[...]).astype(BF16)

    def attend_back(p):
        for h in range(heads):
            mixed = dob_s[p, :, head(h)]
            attention = pf[p, h]
            value_cot = dot_last(mixed, kvw[p, :, head(h, 1)])
            centre = jnp.sum(attention * value_cot, axis=-1, keepdims=True)
            score_grad = (attention * (value_cot - centre) * (ls_ref[0, h] / HS)).astype(BF16)
            dqn[p, :, head(h)] = dot(score_grad, kvw[p, :, head(h)])
            key_grad = dot_first(score_grad, qb_s[p, :, head(h)])
            value_grad = dot_first(attention.astype(BF16), mixed)
            for part, grad in ((0, key_grad), (1, value_grad)):
                hb[p, 0:WIN, head(h, part)] = grad[0:WIN].astype(BF16)
                hb[p, WIN : 2 * WIN, head(h, part)] = grad[rows + WIN :].astype(BF16)
                dkv[p, :, head(h, part)] = grad[WIN : WIN + rows]
        send(hb.at[p, pl.ds(0, WIN)], din.at[p, pl.ds(rows - WIN, WIN)], halo_s.at[p, 2], halo_r.at[p, 2], {"tok": left})
        send(hb.at[p, pl.ds(WIN, WIN)], din.at[p, pl.ds(0, WIN)], halo_s.at[p, 3], halo_r.at[p, 3], {"tok": right})

    def back_wait(p):
        arrived(din.at[p, pl.ds(rows - WIN, WIN)], halo_r.at[p, 2])
        arrived(din.at[p, pl.ds(0, WIN)], halo_r.at[p, 3])

    def unit_back(grad, values):
        one, scale = unit(values)
        return scale * (grad - one * jnp.mean(grad * one, axis=-1, keepdims=True))

    def join_back(p):
        for h in range(heads):
            joined[:, head(h)] = unit_back(dqn[p, :, head(h)], projq[p, :, head(h)]).astype(BF16)
            key_grad = dkv[p, :, head(h)] + din[p, :, head(h)].astype(F32)
            joined[:, head(h, 1)] = unit_back(key_grad, projkv[p, own, head(h)]).astype(BF16)
            joined[:, head(h, 2)] = (dkv[p, :, head(h, 1)] + din[p, :, head(h, 1)].astype(F32)).astype(BF16)

    def product_back():
        return dot_last(joined[...], wq[...])

    def project_back(p, bottom_cot, inverse):
        join_back(p)
        return bottom_cot + norm_back(product_back(), gain_f, scf[p], inverse)

    def pass_on(k):
        send(sx.at[k], nx.at[k], sec_s.at[k], sec_r.at[k], {"section": s_prev})

    with stage("start"):
        for copy in loads:
            copy.start()
        z_own(0, wq, wq_in)
        locals_ = [x_own(0, wq, wq_in)]
        z_own(1, wo, wo_in)
        locals_.append(x_own(1, wo, wo_in))
    with stage("load"):
        for copy in loads:
            copy.wait()
        meta_s[0:1] = ids_v[...].astype(F32)
        meta_s[1:2] = order_v[...].astype(F32)
        meta_s[2:8] = jnp.zeros((6, meta_s.shape[1]), F32)
    gain_f, gain_g = gf_ref[...], gg_ref[...]
    with stage("adapter_fwd1"):
        mask1, dist1 = tables(meta_s[...])
        inv_g1 = adapter_forward(0, a1_ref[...], a2_ref[...], mask1)
        sx[1] = x2s[0].astype(BF16)
        inv_f1 = attention_norm(0)
        norm_halo()
    with stage("adapter_bwd1"):
        adapter_backward(0, g1_ref[...].astype(F32), g2_ref[...], mask1, inv_g1)
        sx[2] = zb_s[0]
    for k in range(1, nz):
        with stage(f"zq{k}"):
            z_step(0, wq, k)
        with stage(f"zo{k}"):
            z_step(1, wo, k, k == 1)
        with stage(f"xq{k - 1}"):
            x_forward(0, wq, k - 1)
    send(meta_s, nmeta, sec_s.at[4], sec_r.at[4], {"section": s_prev})
    with stage("xq_last"):
        x_forward(0, wq, nz - 1)
    x_rest(1, wo)
    pass_on(1)
    pass_on(2)
    with stage("part0"):
        locals_[0].wait()
        norm_halo_wait()
        from_partner(0, wq, 0)
    with stage("qkv_a"):
        qkv_block(x, True)
    with stage("part12"):
        from_partner(0, wq, 1)
        qkv_block(xm, False)
        from_partner(0, wq, 2)
        qkv_block(xp, False)
    with stage("halves"):
        halves(0, wq)
    with stage("part34"):
        from_partner(0, wq, 3)
        from_partner(0, wq, 4)
    with stage("qkv_b"):
        qkv_block(xo, False)
    with stage("kv1"):
        keys_values(0)
        queries(0)
    with stage("xo"):
        x_forward(1, wo)
    with stage("attend1"):
        attend(0, dist1)
    with stage("halves_o"):
        halves(1, wo)
    with stage("part_o"):
        locals_[1].wait()
        for kind in range(5):
            from_partner(1, wo, kind)
    with stage("out1"):
        sx[0] = (a1_ref[...] - dot(ob[0], wo[...])).astype(BF16)
        pass_on(0)
    with stage("dob1"):
        mixed_back(0)
    with stage("attend_back1"):
        attend_back(0)
    flag = (s < ns - 1).astype(F32)
    with stage("sec_wait"):
        arrived(nmeta, sec_r.at[4])
        arrived(nx.at[1], sec_r.at[1])
        arrived(nx.at[0], sec_r.at[0])
    with stage("adapter_fwd2"):
        mask2, dist2 = tables(nmeta[...] * flag)
        top2 = nx[0].astype(F32) * flag
        inv_g2 = adapter_forward(1, top2, nx[1].astype(F32) * flag, mask2)
        inv_f2 = attention_norm(1)
        store(x2s.at[1], o_x2, 1)
    with stage("kv2"):
        kv_whole()
        keys_values(1)
    with stage("q2"):
        q_whole()
        queries(1)
    with stage("back_wait1"):
        back_wait(0)
    with stage("project_back1"):
        sx[3] = project_back(0, g2_ref[...].astype(F32), inv_f1).astype(BF16)
        pass_on(3)

    with stage("halo2"):
        halo_wait(1)
    with stage("attend2"):
        attend(1, dist2)
    with stage("out2"):
        x1_v[...] = top2 - dot(ob[1], wo[...])
        store(x1_v, o_x1, 0)
    with stage("sec_wait2"):
        arrived(nx.at[2], sec_r.at[2])
        arrived(nx.at[3], sec_r.at[3])
    with stage("adapter_bwd2"):
        cot2 = nx[3] * flag.astype(BF16)
        adapter_backward(1, nx[2].astype(F32) * flag, cot2, mask2, inv_g2)
        store(zb_s.at[1], o_d1, 2)

    streams = 2
    srows = d // streams
    xrows = srows // NX
    zrows = xrows // nz
    z_at, back_at = NX, NX + nz - 1
    x_at = back_at + nz - 1
    p_at = x_at + NX - 1

    def srow(h):
        return slice(h * srows, (h + 1) * srows)

    def xpart(h, k):
        return pl.ds(pl.multiple_of(h * srows + k * xrows, xrows), xrows)

    def fpart(h, xx, zz):
        return pl.ds(pl.multiple_of(h * srows + xx * xrows + zz * zrows, zrows), zrows)

    def lane(h, i):
        return ar_s.at[h, i], ar_r.at[h, i]

    def sum_start(h):
        g_s1[srow(h)] = grads[1 - c, srow(h)].astype(BF16)
        at = pl.ds(h * srows, srows)
        send(g_s1.at[at], g_r1.at[at], *lane(h, 0), {"tok": partner})

    def sum_x(h):
        arrived(g_r1.at[pl.ds(h * srows, srows)], ar_r.at[h, 0])
        total = grads[c, srow(h)] + g_r1[srow(h)].astype(F32)
        g_h[srow(h)] = total
        g_s2[srow(h)] = total.astype(BF16)
        for k in (2, 1, 3):
            to = lax.rem(x + k, NX)
            send(g_s2.at[xpart(h, to)], g_r2.at[h, k - 1], *lane(h, k), {"tok": tok_of(to, z, c)})

    def sum_z(h):
        total = g_h[xpart(h, x)]
        for k in range(1, NX):
            arrived(g_r2.at[h, k - 1], ar_r.at[h, k])
        for k in range(1, NX):
            total = total + g_r2[h, k - 1].astype(F32)
        g_q[h] = total
        g_s3[h] = total.astype(BF16)
        for k in range(1, nz):
            to = lax.rem(z + k, nz)
            at = pl.ds(pl.multiple_of(to * zrows, zrows), zrows)
            send(g_s3.at[h, at], g_r3.at[h, k - 1], *lane(h, z_at + k - 1), {"tok": tok_of(x, to, c)})

    def sum_end(h):
        for k in range(1, nz):
            arrived(g_r3.at[h, k - 1], ar_r.at[h, z_at + k - 1])
        total = g_q[h, pl.ds(pl.multiple_of(z * zrows, zrows), zrows)]
        for k in range(1, nz):
            total = total + g_r3[h, k - 1].astype(F32)
        g_out[c, fpart(h, x, z)] = total.astype(BF16)
        mine = g_out.at[c, fpart(h, x, z)]
        for k in range(1, nz):
            to = lax.rem(z + k, nz)
            send(mine, mine, *lane(h, back_at + k - 1), {"tok": tok_of(x, to, c)})

    def share_x(h):
        for k in range(1, nz):
            came = lax.rem(z + nz - k, nz)
            arrived(g_out.at[c, fpart(h, x, came)], ar_r.at[h, back_at + k - 1])
        mine = g_out.at[c, xpart(h, x)]
        for k in (2, 1, 3):
            to = lax.rem(x + k, NX)
            send(mine, mine, *lane(h, x_at + k - 1), {"tok": tok_of(to, z, c)})
        send(mine, mine, *lane(h, p_at), {"tok": partner})

    def share_core(h):
        for k in (1, 3, 2):
            came = g_out.at[c, xpart(h, lax.rem(x + NX - k, NX))]
            arrived(came, ar_r.at[h, x_at + k - 1])
            send(came, came, *lane(h, p_at + k), {"tok": partner})

    def share_end(h):
        for k in range(NX):
            arrived(g_out.at[1 - c, xpart(h, lax.rem(x + NX - k, NX))], ar_r.at[h, p_at + k])

    both = range(streams)
    with stage("ar0"):
        for h in both:
            sum_start(h)
    with stage("dob2"):
        mixed_back(1)
    with stage("ar1"):
        for h in both:
            sum_x(h)
    with stage("attend_back2"):
        attend_back(1)
    with stage("ar2"):
        for h in both:
            sum_z(h)
    with stage("back_wait2"):
        back_wait(1)
    with stage("join2"):
        join_back(1)
    with stage("ar3"):
        for h in both:
            sum_end(h)
    with stage("project_back2"):
        back = product_back()
    with stage("norm_back2"):
        d2_v[...] = (cot2.astype(F32) + norm_back(back, gain_f, scf[1], inv_f2)).astype(BF16)
        store(d2_v, o_d2, 3)
    with stage("ar4"):
        for h in both:
            share_x(h)
    with stage("ar5"):
        for h in both:
            share_core(h)
    with stage("ar6"):
        for h in both:
            share_end(h)
        store(g_out.at[0], o_down, 4)
        for b in range(d // sr):
            up_v[:, b * sr : (b + 1) * sr] = g_out[1, b * sr : (b + 1) * sr]
        store(up_v, o_up, 5)
    with stage("drain"):
        for copy, cond in waits:
            guarded(cond, copy.wait_send)
        for copy in stores:
            copy.wait()


def on_device(
    nz,
    stream_one,
    stream_two,
    grad_one,
    grad_two,
    sensor_ids,
    block_order,
    qkv_weight,
    out_weight,
    attn_gain,
    adapt_gain,
    logit_scale,
    distance_slope,
    adapt_down,
    adapt_up,
):
    ns, nt = lax.axis_size("section"), lax.axis_size("tok")
    rows, d = stream_one.shape[1:]
    sr, heads = adapt_down.shape[2], logit_scale.shape[1]
    blocks = sensor_ids.shape[1]
    span = rows + 2 * WIN
    nflow = 2 * nz - 1
    xrows = d // (2 * NX)
    hbm = pl.BlockSpec(memory_space=pltpu.HBM)
    dma = pltpu.SemaphoreType.DMA
    nar = 1 + 2 * (NX - 1) + 2 * (nz - 1) + NX
    scratch = [
        pltpu.VMEM((d, 3 * d), BF16),
        pltpu.VMEM((d, d), BF16),
        pltpu.VMEM((2, rows, d), F32),
        pltpu.VMEM((2, rows, d), F32),
        pltpu.VMEM((2, rows, d), F32),
        pltpu.VMEM((2, rows, d), BF16),
        pltpu.VMEM((2, rows, sr), F32),
        pltpu.VMEM((2, rows, sr), BF16),
        pltpu.VMEM((2, rows, d), BF16),
        pltpu.VMEM((rows, d), BF16),
        pltpu.VMEM((span, d), BF16),
        pltpu.VMEM((2, rows, d), F32),
        pltpu.VMEM((2, span, 2 * d), F32),
        pltpu.VMEM((2, rows, d), BF16),
        pltpu.VMEM((2, span, 2 * d), BF16),
        pltpu.VMEM((2, heads, rows, span), F32),
        pltpu.VMEM((2, rows, d), BF16),
        pltpu.VMEM((2, rows, d), BF16),
        pltpu.VMEM((2, rows, 2 * d), F32),
        pltpu.VMEM((2, rows, d), F32),
        pltpu.VMEM((rows, 3 * d), BF16),
        pltpu.VMEM((2, 2 * WIN, 2 * d), BF16),
        pltpu.VMEM((2, rows, 2 * d), BF16),
        pltpu.VMEM((2, d, sr), F32),
        pltpu.VMEM((4, rows, d), BF16),
        pltpu.VMEM((4, rows, d), BF16),
        pltpu.VMEM((8, blocks), F32),
        pltpu.VMEM((d, sr), BF16),
        pltpu.VMEM((d, sr), BF16),
        pltpu.VMEM((d, sr), F32),
        pltpu.VMEM((d, sr), BF16),
        pltpu.VMEM((2, NX - 1, xrows, sr), BF16),
        pltpu.VMEM((2, xrows, sr), F32),
        pltpu.VMEM((2, xrows, sr), BF16),
        pltpu.VMEM((2, nz - 1, xrows // nz, sr), BF16),
        pltpu.VMEM((2, d, sr), BF16),
        dma((2, 2, nz)),
        dma((2, 2, nz)),
        dma((2, 2, nflow)),
        dma((2, 2, nflow)),
        dma((2, 2, nflow)),
        dma((2, 2, nflow)),
        dma((2, 5, nflow)),
        dma((2, 5, nflow)),
        dma((2,)),
        dma((2, 4)),
        dma((2, 4)),
        dma((5,)),
        dma((5,)),
        dma((2, nar)),
        dma((2, nar)),
        pltpu.VMEM((rows, d), F32),
        pltpu.VMEM((rows, d), F32),
        pltpu.VMEM((rows, d), BF16),
        pltpu.VMEM((rows, d), BF16),
        pltpu.VMEM((1, blocks), jnp.int32),
        pltpu.VMEM((1, blocks), jnp.int32),
        pltpu.VMEM((1, d), F32),
        pltpu.VMEM((1, d), F32),
        pltpu.VMEM((d, sr), BF16),
        pltpu.VMEM((sr, d), BF16),
        pltpu.VMEM((8, blocks), F32),
        pltpu.VMEM((rows, d), F32),
        pltpu.VMEM((rows, d), BF16),
        pltpu.VMEM((sr, d), BF16),
        pltpu.SMEM((1, heads), F32),
        pltpu.SMEM((1, heads), F32),
        dma((12,)),
        dma((6,)),
    ]
    big = (
        stream_one[0],
        stream_two[0],
        grad_one[0],
        grad_two[0],
        sensor_ids,
        block_order,
        qkv_weight[0],
        out_weight[0],
        attn_gain,
        adapt_gain,
        logit_scale,
        distance_slope,
        adapt_down[0],
        adapt_up[0],
    )
    outs = pl.pallas_call(
        functools.partial(kernel_body, (ns, nt, nz, rows, d, sr, heads)),
        out_shape=(
            jax.ShapeDtypeStruct((rows, d), F32),
            jax.ShapeDtypeStruct((rows, d), F32),
            jax.ShapeDtypeStruct((rows, d), BF16),
            jax.ShapeDtypeStruct((rows, d), BF16),
            jax.ShapeDtypeStruct((d, sr), BF16),
            jax.ShapeDtypeStruct((sr, d), BF16),
        ),
        in_specs=[hbm] * 14,
        out_specs=[hbm] * 6,
        scratch_shapes=scratch,
        compiler_params=pltpu.CompilerParams(
            collective_id=0, has_side_effects=True, vmem_limit_bytes=48 << 20
        ),
    )(
        *(pltpu.with_memory_space_constraint(arr, pltpu.HBM) for arr in big),
    )
    return tuple(out[None] for out in put_out(outs))


def put_out(values):
    def body(*refs):
        n = len(values)
        copies = [pltpu.make_async_copy(refs[i], refs[n + i], refs[2 * n].at[i]) for i in range(n)]
        for copy in copies:
            copy.start()
        for copy in copies:
            copy.wait()

    anywhere = pl.BlockSpec(memory_space=pl.ANY)
    return pl.pallas_call(
        body,
        out_shape=tuple(pltpu.HBM(v.shape, v.dtype) for v in values),
        in_specs=[anywhere] * len(values),
        out_specs=[pl.BlockSpec(memory_space=pltpu.HBM)] * len(values),
        scratch_shapes=[pltpu.SemaphoreType.DMA((len(values),))],
        compiler_params=pltpu.CompilerParams(vmem_limit_bytes=1 << 20),
    )(*values)


def solution(mesh):
    three, two = P("section", "tok", None), P("section", None)
    whole = P("section", None, None)
    in_specs = (three,) * 4 + (two,) * 2 + (three,) * 2 + (two,) * 4 + (whole,) * 2
    out_specs = (three,) * 4 + (whole,) * 2
    nz = mesh.shape["tok"] // (2 * NX)
    return jax.shard_map(
        functools.partial(on_device, nz),
        mesh=mesh,
        in_specs=in_specs,
        out_specs=out_specs,
        check_vma=False,
    )
```

```python
import contextlib
import functools

import jax
import jax.numpy as jnp
from jax import lax
from jax.experimental import pallas as pl
from jax.experimental.pallas import tpu as pltpu
from jax.sharding import PartitionSpec as P

RANK = 16
BLOCK = 16
WIN = 32
HS = 128
NX = 4
MESH = pl.DeviceIdType.MESH
F32 = jnp.float32
BF16 = jnp.bfloat16


def stage(name):
    return contextlib.nullcontext()


def dot(left, right):
    return jnp.dot(left, right, preferred_element_type=F32)


def dot_last(left, right):
    return lax.dot_general(left, right, (((1,), (1,)), ((), ())), preferred_element_type=F32)


def dot_first(left, right):
    return lax.dot_general(left, right, (((0,), (0,)), ((), ())), preferred_element_type=F32)


def layer_norm(values):
    centred = values - jnp.mean(values, axis=-1, keepdims=True)
    inverse = lax.rsqrt(jnp.mean(centred * centred, axis=-1, keepdims=True) + 1e-05)
    return centred * inverse, inverse


def norm_back(upstream, gain, scaled, inverse):
    inner = upstream * gain
    mean_one = jnp.mean(inner, axis=-1, keepdims=True)
    mean_two = jnp.mean(inner * scaled, axis=-1, keepdims=True)
    return inverse * (inner - mean_one - scaled * mean_two)


def phi(values):
    return 0.5 * (1.0 + lax.erf(values * 0.7071067811865476))


def kernel_body(sizes, *refs):
    ns, nt, nz, rows, d, sr, heads = sizes
    span = rows + 2 * WIN
    (
        a1_in, a2_in, g1_in, g2_in, ids_in, order_in, wq_in, wo_in, gf_in, gg_in,
        ls_in, sl_in, down_in, up_in,
        o_x1, o_x2, o_d1, o_d2, o_down, o_up,
        wq, wo, x2s, scg, scf, na_s, pre_s, hid_s, zb_s, nf_s, nfw, projq, projkv, qb_s, kvw, pf, ob, dob_s,
        dkv, dqn, joined, hb, din, grads,
        sx, nx, nmeta,
        g_s1, g_r1, g_h, g_s2, g_r2, g_q, g_s3, g_r3, g_out,
        zs, zr, xs, xr, hs, hr, ps, pr, lsem,
        halo_s, halo_r, sec_s, sec_r, ar_s, ar_r,
        a1_ref, a2_ref, g1_ref, g2_ref, ids_v, order_v, gf_ref, gg_ref, down_ref, up_ref,
        meta_s, x1_v, d2_v, up_v, ls_ref, sl_ref, load_sem, store_sem,
    ) = refs
    moves = (
        (a1_in, a1_ref), (ids_in, ids_v), (order_in, order_v), (gg_in, gg_ref), (down_in, down_ref), (up_in, up_ref),
        (a2_in, a2_ref), (gf_in, gf_ref), (g1_in, g1_ref), (g2_in, g2_ref), (ls_in, ls_ref), (sl_in, sl_ref),
    )
    loads = [pltpu.make_async_copy(a, b, load_sem.at[i]) for i, (a, b) in enumerate(moves)]
    stores = []

    def store(src, dst, i):
        copy = pltpu.make_async_copy(src, dst, store_sem.at[i])
        copy.start()
        stores.append(copy)

    s = lax.axis_index("section")
    t = lax.axis_index("tok")
    c = lax.rem(t, 2)
    z = lax.rem(t // 2, nz)
    x = t // (2 * nz)
    nchip = 2 * nz

    def tok_of(xx, zz, cc):
        return (xx * nz + zz) * 2 + cc

    partner = tok_of(x, z, 1 - c)
    xp, xm, xo = lax.rem(x + 1, NX), lax.rem(x + NX - 1, NX), lax.rem(x + 2, NX)
    right, left = lax.rem(t + 1, nt), lax.rem(t + nt - 1, nt)
    s_next, s_prev = lax.rem(s + 1, ns), lax.rem(s + ns - 1, ns)

    barrier = pltpu.get_barrier_semaphore()
    greet = [partner, left, right]
    greet += [tok_of(lax.rem(x + k, NX), z, c) for k in range(1, NX)]
    greet += [tok_of(x, lax.rem(z + k, nz), c) for k in range(1, nz)]
    for other in greet:
        pl.semaphore_signal(barrier, inc=1, device_id={"tok": other}, device_id_type=MESH)
    for other in (s_next, s_prev):
        pl.semaphore_signal(barrier, inc=1, device_id={"section": other}, device_id_type=MESH)
    pl.semaphore_wait(barrier, len(greet) + 2)

    waits = []

    def send(src, dst, ssem, rsem, where, cond=None):
        copy = pltpu.make_async_remote_copy(
            src_ref=src, dst_ref=dst, send_sem=ssem, recv_sem=rsem,
            device_id=where, device_id_type=MESH,
        )
        if cond is None:
            copy.start()
        else:
            pl.when(cond)(copy.start)
        waits.append((copy, cond))

    def arrived(dst, rsem):
        pltpu.make_async_remote_copy(
            src_ref=dst, dst_ref=dst, send_sem=rsem, recv_sem=rsem,
            device_id={"tok": partner}, device_id_type=MESH,
        ).wait_recv()

    shard = d // nt
    half = shard // 2
    flows = [(z, None, 0, 0)]
    for k in range(1, nz):
        flows.append((z - k, z - k >= 0, 1, k))
    for k in range(1, nz):
        flows.append((z + k, z + k <= nz - 1, -1, k))
    nf_ = len(flows)

    def place(w, xx, zz, part=None):
        base = tok_of(xx, zz, c) * shard
        if part is None:
            return w.at[pl.ds(pl.multiple_of(base, shard), shard)]
        return w.at[pl.ds(pl.multiple_of(base + part * half, half), half)]

    def place_of(w, xx, zz, cc, part=None):
        base = tok_of(xx, zz, cc) * shard
        if part is None:
            return w.at[pl.ds(pl.multiple_of(base, shard), shard)]
        return w.at[pl.ds(pl.multiple_of(base + part * half, half), half)]

    def spread(i, w, src, f, zf, cond):
        dst = place(w, x, zf)
        send(src, dst, xs.at[i, 0, f], xr.at[i, 0, f], {"tok": tok_of(xp, z, c)}, cond)
        send(src, dst, xs.at[i, 1, f], xr.at[i, 1, f], {"tok": tok_of(xm, z, c)}, cond)
        send(src, dst, ps.at[i, 0, f], pr.at[i, 0, f], {"tok": partner}, cond)

    def clip(v):
        return jnp.clip(v, 0, nz - 1)

    def z_own(i, w, w_in):
        if nz > 1:
            dst = place(w, x, z)
            send(w_in, dst, zs.at[i, 0, 0], zr.at[i, 0, 1], {"tok": tok_of(x, clip(z + 1), c)}, z < nz - 1)
            send(w_in, dst, zs.at[i, 1, 0], zr.at[i, 1, 1], {"tok": tok_of(x, clip(z - 1), c)}, z > 0)

    def x_own(i, w, w_in):
        spread(i, w, w_in, 0, z, None)
        local = pltpu.make_async_copy(w_in, place(w, x, z), lsem.at[i])
        local.start()
        return local

    def z_step(i, w, k, onward=True):
        for way, (f, step) in enumerate(((k, 1), (nz - 1 + k, -1))):
            zf, cond = flows[f][0], flows[f][1]
            zc = clip(zf)
            dst = place(w, x, zc)
            pl.when(cond)(functools.partial(arrived, dst, zr.at[i, way, k]))
            if k < nz - 1:
                inside = z < nz - 1 if way == 0 else z > 0
                send(dst, dst, zs.at[i, way, k], zr.at[i, way, k + 1], {"tok": tok_of(x, clip(z + step), c)},
                     jnp.logical_and(cond, inside))
            if onward:
                spread(i, w, dst, f, zc, cond)

    def x_rest(i, w):
        for f, zf, cond in each_flow():
            if f not in (0, 1, nz):
                spread(i, w, place(w, x, zf), f, zf, cond)

    def each_flow(only=None):
        for k in range(nf_):
            f = (k + 1) // 2 + (nz - 1) * (k > 0 and k % 2 == 0)
            if only is not None and (k + 1) // 2 != only:
                continue
            zf, cond = flows[f][0], flows[f][1]
            yield f, jnp.clip(zf, 0, nz - 1), cond

    def guarded(cond, fn):
        if cond is None:
            fn()
        else:
            pl.when(cond)(fn)

    def x_forward(i, w, only=None):
        for f, zf, cond in each_flow(only):
            for way, (origin, onward) in enumerate(((xm, xp), (xp, xm))):
                dst = place(w, origin, zf)
                guarded(cond, functools.partial(arrived, dst, xr.at[i, way, f]))
                piece = place(w, origin, zf, way)
                send(piece, piece, hs.at[i, way, f], hr.at[i, way, f], {"tok": tok_of(onward, z, c)}, cond)
                send(dst, dst, ps.at[i, 1 + way, f], pr.at[i, 1 + way, f], {"tok": partner}, cond)

    def halves(i, w):
        for f, zf, cond in each_flow():
            for way in range(2):
                piece = place(w, xo, zf, way)
                guarded(cond, functools.partial(arrived, piece, hr.at[i, way, f]))
                send(piece, piece, ps.at[i, 3 + way, f], pr.at[i, 3 + way, f], {"tok": partner}, cond)

    def from_partner(i, w, kind):
        for f, zf, cond in each_flow():
            origin = (x, xm, xp, xo, xo)[kind]
            dst = place_of(w, origin, zf, 1 - c, kind - 3 if kind >= 3 else None)
            guarded(cond, functools.partial(arrived, dst, pr.at[i, kind, f]))

    def tables(meta):
        row_block = lax.broadcasted_iota(jnp.int32, (rows, meta.shape[1]), 0) // BLOCK + t * (rows // BLOCK)
        pick = (lax.broadcasted_iota(jnp.int32, (rows, meta.shape[1]), 1) == row_block).astype(BF16)
        per_row = dot_last(pick, meta.astype(BF16))
        sensor, spot = per_row[:, 0:1], per_row[:, 1:2]
        first = t * (rows // BLOCK) - WIN // BLOCK
        key_block = lax.broadcasted_iota(jnp.int32, (meta.shape[1], span), 1) // BLOCK + first
        pick_key = (lax.broadcasted_iota(jnp.int32, (meta.shape[1], span), 0) == key_block).astype(BF16)
        key_spot = dot(meta.astype(BF16), pick_key)[1:2, :]
        owner = (lax.broadcasted_iota(jnp.int32, (rows, sr), 1) // RANK).astype(F32)
        mask = (owner == sensor).astype(F32)
        distance = jnp.log(1.0 + jnp.abs(spot - key_spot))
        return mask, distance

    q_idx = lax.broadcasted_iota(jnp.int32, (rows, span), 0)
    k_idx = lax.broadcasted_iota(jnp.int32, (rows, span), 1)
    key_at = k_idx + (t * rows - WIN)
    allowed = (
        (k_idx >= q_idx) & (k_idx <= q_idx + 2 * WIN) & (key_at >= 0) & (key_at < nt * rows)
    ).astype(F32)

    def adapter_forward(p, top, bottom, mask):
        scaled, inverse = layer_norm(top)
        scg[p] = scaled
        adapt_in = (scaled * gain_g).astype(BF16)
        na_s[p] = adapt_in
        pre = dot(adapt_in, down_ref[...]) * mask
        pre_s[p] = pre
        hidden = (pre * phi(pre)).astype(BF16)
        hid_s[p] = hidden
        x2s[p] = bottom - dot(hidden, up_ref[...])
        return inverse

    def adapter_grads(p, bottom_cot, mask):
        pre = pre_s[p]
        slope = phi(pre) + pre * jnp.exp(-0.5 * pre * pre) * 0.3989422804014327
        cot = dot_last(bottom_cot, up_ref[...])
        hidden_grad = (mask * slope * cot).astype(BF16)
        grad_down = dot_first(na_s[p], hidden_grad)
        grad_up = dot_first(hid_s[p], bottom_cot)
        if p == 0:
            grads[0] = grad_down
        else:
            grads[0] = grads[0] + grad_down
        for b in range(d // sr):
            part = grad_up[:, b * sr : (b + 1) * sr]
            at = slice(b * sr, (b + 1) * sr)
            grads[1, at] = part if p == 0 else grads[1, at] + part
        return hidden_grad

    def adapter_cot(p, top_cot, hidden_grad, inverse):
        back = dot_last(hidden_grad, down_ref[...])
        zb_s[p] = (top_cot + norm_back(back, gain_g, scg[p], inverse)).astype(BF16)

    def attention_norm(p):
        scaled, inverse = layer_norm(x2s[p])
        scf[p] = scaled
        if p == 0:
            nfw[WIN : WIN + rows] = (scaled * gain_f).astype(BF16)
        else:
            nf_s[...] = (scaled * gain_f).astype(BF16)
        return inverse

    kblock = d // NX

    def qkv_block(xx, first):
        at = pl.ds(pl.multiple_of(xx * kblock, kblock), kblock)
        part = dot(nfw[WIN : WIN + rows, at], wq[at, 0:d])
        projq[0] = part if first else projq[0] + part
        for n in range(2):
            cols = slice(n * d, (n + 1) * d)
            part = dot(nfw[:, at], wq[at, (n + 1) * d : (n + 2) * d])
            projkv[0, :, cols] = part if first else projkv[0, :, cols] + part

    own = slice(WIN, WIN + rows)

    def kv_whole():
        for n in range(2):
            projkv[1, own, n * d : (n + 1) * d] = dot(nf_s[...], wq[:, (n + 1) * d : (n + 2) * d])

    def q_whole():
        projq[1] = dot(nf_s[...], wq[:, 0:d])

    def unit(values):
        scale = lax.rsqrt(jnp.mean(values * values, axis=-1, keepdims=True) + 1e-06)
        return values * scale, scale

    def head(h, part=0):
        return slice(part * d + h * HS, part * d + (h + 1) * HS)

    def keys_values(p):
        at = own if p else slice(0, span)
        for h in range(heads):
            kvw[p, at, head(h)] = unit(projkv[p, at, head(h)])[0].astype(BF16)
            kvw[p, at, head(h, 1)] = projkv[p, at, head(h, 1)].astype(BF16)
        if p:
            first = kvw.at[p, pl.ds(WIN, WIN)]
            last = kvw.at[p, pl.ds(rows, WIN)]
            send(first, kvw.at[p, pl.ds(rows + WIN, WIN)], halo_s.at[p, 0], halo_r.at[p, 0], {"tok": left})
            send(last, kvw.at[p, pl.ds(0, WIN)], halo_s.at[p, 1], halo_r.at[p, 1], {"tok": right})

    def norm_halo():
        first = nfw.at[pl.ds(WIN, WIN)]
        last = nfw.at[pl.ds(rows, WIN)]
        send(first, nfw.at[pl.ds(rows + WIN, WIN)], halo_s.at[0, 0], halo_r.at[0, 0], {"tok": left})
        send(last, nfw.at[pl.ds(0, WIN)], halo_s.at[0, 1], halo_r.at[0, 1], {"tok": right})

    def norm_halo_wait():
        arrived(nfw.at[pl.ds(rows + WIN, WIN)], halo_r.at[0, 0])
        arrived(nfw.at[pl.ds(0, WIN)], halo_r.at[0, 1])

    def halo_wait(p):
        arrived(kvw.at[p, pl.ds(rows + WIN, WIN)], halo_r.at[p, 0])
        arrived(kvw.at[p, pl.ds(0, WIN)], halo_r.at[p, 1])

    def queries(p):
        for h in range(heads):
            qb_s[p, :, head(h)] = unit(projq[p, :, head(h)])[0].astype(BF16)

    def attend(p, distance):
        for h in range(heads):
            score = dot_last(qb_s[p, :, head(h)], kvw[p, :, head(h)])
            score = score * (ls_ref[0, h] / HS) - sl_ref[0, h] * distance
            weights = jnp.exp(score) * allowed
            attention = weights / jnp.sum(weights, axis=-1, keepdims=True)
            pf[p, h] = attention
            ob[p, :, head(h)] = dot(attention.astype(BF16), kvw[p, :, head(h, 1)]).astype(BF16)

    def mixed_back(p):
        dob_s[p] = dot_last(zb_s[p], wo[...]).astype(BF16)

    def attend_back(p):
        for h in range(heads):
            mixed = dob_s[p, :, head(h)]
            attention = pf[p, h]
            value_cot = dot_last(mixed, kvw[p, :, head(h, 1)])
            centre = jnp.sum(attention * value_cot, axis=-1, keepdims=True)
            score_grad = (attention * (value_cot - centre) * (ls_ref[0, h] / HS)).astype(BF16)
            dqn[p, :, head(h)] = dot(score_grad, kvw[p, :, head(h)])
            key_grad = dot_first(score_grad, qb_s[p, :, head(h)])
            value_grad = dot_first(attention.astype(BF16), mixed)
            for part, grad in ((0, key_grad), (1, value_grad)):
                hb[p, 0:WIN, head(h, part)] = grad[0:WIN].astype(BF16)
                hb[p, WIN : 2 * WIN, head(h, part)] = grad[rows + WIN :].astype(BF16)
                dkv[p, :, head(h, part)] = grad[WIN : WIN + rows]
        send(hb.at[p, pl.ds(0, WIN)], din.at[p, pl.ds(rows - WIN, WIN)], halo_s.at[p, 2], halo_r.at[p, 2], {"tok": left})
        send(hb.at[p, pl.ds(WIN, WIN)], din.at[p, pl.ds(0, WIN)], halo_s.at[p, 3], halo_r.at[p, 3], {"tok": right})

    def back_wait(p):
        arrived(din.at[p, pl.ds(rows - WIN, WIN)], halo_r.at[p, 2])
        arrived(din.at[p, pl.ds(0, WIN)], halo_r.at[p, 3])

    def unit_back(grad, values):
        one, scale = unit(values)
        return scale * (grad - one * jnp.mean(grad * one, axis=-1, keepdims=True))

    def join_queries(p):
        for h in range(heads):
            joined[:, head(h)] = unit_back(dqn[p, :, head(h)], projq[p, :, head(h)]).astype(BF16)
        return dot_last(joined[:, 0:d], wq[:, 0:d])

    def join_back(p):
        for h in range(heads):
            key_grad = dkv[p, :, head(h)] + din[p, :, head(h)].astype(F32)
            joined[:, head(h, 1)] = unit_back(key_grad, projkv[p, own, head(h)]).astype(BF16)
            joined[:, head(h, 2)] = (dkv[p, :, head(h, 1)] + din[p, :, head(h, 1)].astype(F32)).astype(BF16)

    def product_back(part):
        return part + dot_last(joined[:, d:], wq[:, d:])

    def pass_on(k):
        send(sx.at[k], nx.at[k], sec_s.at[k], sec_r.at[k], {"section": s_prev})

    with stage("start"):
        for copy in loads:
            copy.start()
        z_own(0, wq, wq_in)
        locals_ = [x_own(0, wq, wq_in)]
        z_own(1, wo, wo_in)
        locals_.append(x_own(1, wo, wo_in))
    with stage("load"):
        for copy in loads:
            copy.wait()
        meta_s[0:1] = ids_v[...].astype(F32)
        meta_s[1:2] = order_v[...].astype(F32)
        meta_s[2:8] = jnp.zeros((6, meta_s.shape[1]), F32)
    gain_f, gain_g = gf_ref[...], gg_ref[...]
    with stage("adapter_fwd1"):
        mask1, dist1 = tables(meta_s[...])
        inv_g1 = adapter_forward(0, a1_ref[...], a2_ref[...], mask1)
        sx[1] = x2s[0].astype(BF16)
        inv_f1 = attention_norm(0)
        norm_halo()
    with stage("adapter_bwd1"):
        hidden1 = adapter_grads(0, g2_ref[...], mask1)
        adapter_cot(0, g1_ref[...].astype(F32), hidden1, inv_g1)
        sx[2] = zb_s[0]
    for k in range(1, nz):
        with stage(f"zq{k}"):
            z_step(0, wq, k)
        with stage(f"zo{k}"):
            z_step(1, wo, k, k == 1)
        with stage(f"xq{k - 1}"):
            x_forward(0, wq, k - 1)
    send(meta_s, nmeta, sec_s.at[4], sec_r.at[4], {"section": s_prev})
    with stage("xq_last"):
        x_forward(0, wq, nz - 1)
    x_rest(1, wo)
    pass_on(1)
    pass_on(2)
    with stage("part0"):
        locals_[0].wait()
        norm_halo_wait()
        from_partner(0, wq, 0)
    with stage("qkv_a"):
        qkv_block(x, True)
    with stage("part12"):
        from_partner(0, wq, 1)
        qkv_block(xm, False)
        from_partner(0, wq, 2)
        qkv_block(xp, False)
    with stage("halves"):
        halves(0, wq)
    with stage("part34"):
        from_partner(0, wq, 3)
        from_partner(0, wq, 4)
    with stage("qkv_b"):
        qkv_block(xo, False)
    with stage("kv1"):
        keys_values(0)
        queries(0)
    with stage("xo"):
        x_forward(1, wo)
    with stage("attend1"):
        attend(0, dist1)
    with stage("halves_o"):
        halves(1, wo)
    with stage("part_o"):
        locals_[1].wait()
        for kind in range(5):
            from_partner(1, wo, kind)
    with stage("out1"):
        sx[0] = (a1_ref[...] - dot(ob[0], wo[...])).astype(BF16)
        pass_on(0)
    with stage("dob1"):
        mixed_back(0)
    with stage("attend_back1"):
        attend_back(0)
    flag = (s < ns - 1).astype(F32)
    with stage("join1"):
        part1 = join_queries(0)
        arrived(nmeta, sec_r.at[4])
        mask2, dist2 = tables(nmeta[...] * flag)
    with stage("sec_wait"):
        arrived(nx.at[1], sec_r.at[1])
        arrived(nx.at[0], sec_r.at[0])
    with stage("adapter_fwd2"):
        top2 = nx[0].astype(F32) * flag
        inv_g2 = adapter_forward(1, top2, nx[1].astype(F32) * flag, mask2)
        inv_f2 = attention_norm(1)
        store(x2s.at[1], o_x2, 1)
    with stage("kv2"):
        kv_whole()
        keys_values(1)
    with stage("q2"):
        q_whole()
        queries(1)
    with stage("back_wait1"):
        back_wait(0)
    with stage("project_back1"):
        join_back(0)
        back = norm_back(product_back(part1), gain_f, scf[0], inv_f1)
        sx[3] = (g2_ref[...].astype(F32) + back).astype(BF16)
        pass_on(3)

    with stage("halo2"):
        halo_wait(1)
    with stage("attend2"):
        attend(1, dist2)
    with stage("out2"):
        x1_v[...] = top2 - dot(ob[1], wo[...])
        store(x1_v, o_x1, 0)
    with stage("sec_wait2"):
        arrived(nx.at[2], sec_r.at[2])
        arrived(nx.at[3], sec_r.at[3])
    with stage("adapter_bwd2"):
        cot2 = nx[3] * flag.astype(BF16)
        hidden2 = adapter_grads(1, cot2, mask2)

    streams = 2
    srows = d // streams
    xrows = srows // NX
    zrows = xrows // nz
    z_at, back_at = NX, NX + nz - 1
    x_at = back_at + nz - 1
    p_at = x_at + NX - 1

    def srow(h):
        return slice(h * srows, (h + 1) * srows)

    def xpart(h, k):
        return pl.ds(pl.multiple_of(h * srows + k * xrows, xrows), xrows)

    def fpart(h, xx, zz):
        return pl.ds(pl.multiple_of(h * srows + xx * xrows + zz * zrows, zrows), zrows)

    def lane(h, i):
        return ar_s.at[h, i], ar_r.at[h, i]

    def sum_start(h):
        g_s1[srow(h)] = grads[1 - c, srow(h)].astype(BF16)
        at = pl.ds(h * srows, srows)
        send(g_s1.at[at], g_r1.at[at], *lane(h, 0), {"tok": partner})

    def sum_x(h):
        arrived(g_r1.at[pl.ds(h * srows, srows)], ar_r.at[h, 0])
        total = grads[c, srow(h)] + g_r1[srow(h)].astype(F32)
        g_h[srow(h)] = total
        g_s2[srow(h)] = total.astype(BF16)
        for k in (2, 1, 3):
            to = lax.rem(x + k, NX)
            send(g_s2.at[xpart(h, to)], g_r2.at[h, k - 1], *lane(h, k), {"tok": tok_of(to, z, c)})

    def sum_z(h):
        total = g_h[xpart(h, x)]
        for k in range(1, NX):
            arrived(g_r2.at[h, k - 1], ar_r.at[h, k])
        for k in range(1, NX):
            total = total + g_r2[h, k - 1].astype(F32)
        g_q[h] = total
        g_s3[h] = total.astype(BF16)
        for k in range(1, nz):
            to = lax.rem(z + k, nz)
            at = pl.ds(pl.multiple_of(to * zrows, zrows), zrows)
            send(g_s3.at[h, at], g_r3.at[h, k - 1], *lane(h, z_at + k - 1), {"tok": tok_of(x, to, c)})

    def sum_end(h):
        for k in range(1, nz):
            arrived(g_r3.at[h, k - 1], ar_r.at[h, z_at + k - 1])
        total = g_q[h, pl.ds(pl.multiple_of(z * zrows, zrows), zrows)]
        for k in range(1, nz):
            total = total + g_r3[h, k - 1].astype(F32)
        g_out[c, fpart(h, x, z)] = total.astype(BF16)
        mine = g_out.at[c, fpart(h, x, z)]
        for k in range(1, nz):
            to = lax.rem(z + k, nz)
            send(mine, mine, *lane(h, back_at + k - 1), {"tok": tok_of(x, to, c)})

    def share_x(h):
        for k in range(1, nz):
            came = lax.rem(z + nz - k, nz)
            arrived(g_out.at[c, fpart(h, x, came)], ar_r.at[h, back_at + k - 1])
        mine = g_out.at[c, xpart(h, x)]
        for k in (2, 1, 3):
            to = lax.rem(x + k, NX)
            send(mine, mine, *lane(h, x_at + k - 1), {"tok": tok_of(to, z, c)})
        send(mine, mine, *lane(h, p_at), {"tok": partner})

    def share_core(h):
        for k in (1, 3, 2):
            came = g_out.at[c, xpart(h, lax.rem(x + NX - k, NX))]
            arrived(came, ar_r.at[h, x_at + k - 1])
            send(came, came, *lane(h, p_at + k), {"tok": partner})

    def share_end(h):
        for k in range(NX):
            arrived(g_out.at[1 - c, xpart(h, lax.rem(x + NX - k, NX))], ar_r.at[h, p_at + k])

    both = range(streams)
    with stage("ar0"):
        for h in both:
            sum_start(h)
    with stage("cot2"):
        adapter_cot(1, nx[2].astype(F32) * flag, hidden2, inv_g2)
        store(zb_s.at[1], o_d1, 2)
    with stage("dob2"):
        mixed_back(1)
    with stage("ar1"):
        for h in both:
            sum_x(h)
    with stage("attend_back2"):
        attend_back(1)
    with stage("ar2"):
        for h in both:
            sum_z(h)
    with stage("join2q"):
        part2 = join_queries(1)
    with stage("back_wait2"):
        back_wait(1)
    with stage("join2"):
        join_back(1)
    with stage("ar3"):
        for h in both:
            sum_end(h)
    with stage("project_back2"):
        back = product_back(part2)
    with stage("norm_back2"):
        d2_v[...] = (cot2.astype(F32) + norm_back(back, gain_f, scf[1], inv_f2)).astype(BF16)
        store(d2_v, o_d2, 3)
    with stage("ar4"):
        for h in both:
            share_x(h)
    with stage("ar5"):
        for h in both:
            share_core(h)
    with stage("ar6"):
        for h in both:
            share_end(h)
        store(g_out.at[0], o_down, 4)
        for b in range(d // sr):
            up_v[:, b * sr : (b + 1) * sr] = g_out[1, b * sr : (b + 1) * sr]
        store(up_v, o_up, 5)
    with stage("drain"):
        for copy, cond in waits:
            guarded(cond, copy.wait_send)
        for copy in stores:
            copy.wait()


def on_device(
    nz,
    stream_one,
    stream_two,
    grad_one,
    grad_two,
    sensor_ids,
    block_order,
    qkv_weight,
    out_weight,
    attn_gain,
    adapt_gain,
    logit_scale,
    distance_slope,
    adapt_down,
    adapt_up,
):
    ns, nt = lax.axis_size("section"), lax.axis_size("tok")
    rows, d = stream_one.shape[1:]
    sr, heads = adapt_down.shape[2], logit_scale.shape[1]
    blocks = sensor_ids.shape[1]
    span = rows + 2 * WIN
    nflow = 2 * nz - 1
    xrows = d // (2 * NX)
    hbm = pl.BlockSpec(memory_space=pltpu.HBM)
    dma = pltpu.SemaphoreType.DMA
    nar = 1 + 2 * (NX - 1) + 2 * (nz - 1) + NX
    scratch = [
        pltpu.VMEM((d, 3 * d), BF16),
        pltpu.VMEM((d, d), BF16),
        pltpu.VMEM((2, rows, d), F32),
        pltpu.VMEM((2, rows, d), F32),
        pltpu.VMEM((2, rows, d), F32),
        pltpu.VMEM((2, rows, d), BF16),
        pltpu.VMEM((2, rows, sr), F32),
        pltpu.VMEM((2, rows, sr), BF16),
        pltpu.VMEM((2, rows, d), BF16),
        pltpu.VMEM((rows, d), BF16),
        pltpu.VMEM((span, d), BF16),
        pltpu.VMEM((2, rows, d), F32),
        pltpu.VMEM((2, span, 2 * d), F32),
        pltpu.VMEM((2, rows, d), BF16),
        pltpu.VMEM((2, span, 2 * d), BF16),
        pltpu.VMEM((2, heads, rows, span), F32),
        pltpu.VMEM((2, rows, d), BF16),
        pltpu.VMEM((2, rows, d), BF16),
        pltpu.VMEM((2, rows, 2 * d), F32),
        pltpu.VMEM((2, rows, d), F32),
        pltpu.VMEM((rows, 3 * d), BF16),
        pltpu.VMEM((2, 2 * WIN, 2 * d), BF16),
        pltpu.VMEM((2, rows, 2 * d), BF16),
        pltpu.VMEM((2, d, sr), F32),
        pltpu.VMEM((4, rows, d), BF16),
        pltpu.VMEM((4, rows, d), BF16),
        pltpu.VMEM((8, blocks), F32),
        pltpu.VMEM((d, sr), BF16),
        pltpu.VMEM((d, sr), BF16),
        pltpu.VMEM((d, sr), F32),
        pltpu.VMEM((d, sr), BF16),
        pltpu.VMEM((2, NX - 1, xrows, sr), BF16),
        pltpu.VMEM((2, xrows, sr), F32),
        pltpu.VMEM((2, xrows, sr), BF16),
        pltpu.VMEM((2, nz - 1, xrows // nz, sr), BF16),
        pltpu.VMEM((2, d, sr), BF16),
        dma((2, 2, nz)),
        dma((2, 2, nz)),
        dma((2, 2, nflow)),
        dma((2, 2, nflow)),
        dma((2, 2, nflow)),
        dma((2, 2, nflow)),
        dma((2, 5, nflow)),
        dma((2, 5, nflow)),
        dma((2,)),
        dma((2, 4)),
        dma((2, 4)),
        dma((5,)),
        dma((5,)),
        dma((2, nar)),
        dma((2, nar)),
        pltpu.VMEM((rows, d), F32),
        pltpu.VMEM((rows, d), F32),
        pltpu.VMEM((rows, d), BF16),
        pltpu.VMEM((rows, d), BF16),
        pltpu.VMEM((1, blocks), jnp.int32),
        pltpu.VMEM((1, blocks), jnp.int32),
        pltpu.VMEM((1, d), F32),
        pltpu.VMEM((1, d), F32),
        pltpu.VMEM((d, sr), BF16),
        pltpu.VMEM((sr, d), BF16),
        pltpu.VMEM((8, blocks), F32),
        pltpu.VMEM((rows, d), F32),
        pltpu.VMEM((rows, d), BF16),
        pltpu.VMEM((sr, d), BF16),
        pltpu.SMEM((1, heads), F32),
        pltpu.SMEM((1, heads), F32),
        dma((12,)),
        dma((6,)),
    ]
    big = (
        stream_one[0],
        stream_two[0],
        grad_one[0],
        grad_two[0],
        sensor_ids,
        block_order,
        qkv_weight[0],
        out_weight[0],
        attn_gain,
        adapt_gain,
        logit_scale,
        distance_slope,
        adapt_down[0],
        adapt_up[0],
    )
    outs = pl.pallas_call(
        functools.partial(kernel_body, (ns, nt, nz, rows, d, sr, heads)),
        out_shape=(
            jax.ShapeDtypeStruct((rows, d), F32),
            jax.ShapeDtypeStruct((rows, d), F32),
            jax.ShapeDtypeStruct((rows, d), BF16),
            jax.ShapeDtypeStruct((rows, d), BF16),
            jax.ShapeDtypeStruct((d, sr), BF16),
            jax.ShapeDtypeStruct((sr, d), BF16),
        ),
        in_specs=[hbm] * 14,
        out_specs=[hbm] * 6,
        scratch_shapes=scratch,
        compiler_params=pltpu.CompilerParams(
            collective_id=0, has_side_effects=True, vmem_limit_bytes=48 << 20
        ),
    )(
        *(pltpu.with_memory_space_constraint(arr, pltpu.HBM) for arr in big),
    )
    return tuple(out[None] for out in put_out(outs))


def put_out(values):
    def body(*refs):
        n = len(values)
        copies = [pltpu.make_async_copy(refs[i], refs[n + i], refs[2 * n].at[i]) for i in range(n)]
        for copy in copies:
            copy.start()
        for copy in copies:
            copy.wait()

    anywhere = pl.BlockSpec(memory_space=pl.ANY)
    return pl.pallas_call(
        body,
        out_shape=tuple(pltpu.HBM(v.shape, v.dtype) for v in values),
        in_specs=[anywhere] * len(values),
        out_specs=[pl.BlockSpec(memory_space=pltpu.HBM)] * len(values),
        scratch_shapes=[pltpu.SemaphoreType.DMA((len(values),))],
        compiler_params=pltpu.CompilerParams(vmem_limit_bytes=1 << 20),
    )(*values)


def solution(mesh):
    three, two = P("section", "tok", None), P("section", None)
    whole = P("section", None, None)
    in_specs = (three,) * 4 + (two,) * 2 + (three,) * 2 + (two,) * 4 + (whole,) * 2
    out_specs = (three,) * 4 + (whole,) * 2
    nz = mesh.shape["tok"] // (2 * NX)
    return jax.shard_map(
        functools.partial(on_device, nz),
        mesh=mesh,
        in_specs=in_specs,
        out_specs=out_specs,
        check_vma=False,
    )
```
